256 devices in a mesh: rows: 8 (over x, core), pts: 32 (over y, z).
Axes of the slice: x: 4, y: 4, z: 8, core: 2. Of those that a mesh axis runs over, the one named last changes fastest.
Arguments:
- features: bfloat16 [32768, 128], P('pts'), may hold values from -6 to 6
- targets: bfloat16 [32768, 256], P('pts'), may hold values from -6 to 6
- coefficients: float32 [32768, 256], P('pts'), may hold values from -6 to 6
- momentum: float32 [32768, 256], P('pts'), may hold values from -6 to 6
- block_index: int32 [2, 2048], replicated, may hold values from 0 to 32767, as said below
- pivot_index: int32 [2, 512], replicated, may hold values from 0 to 2047, as said below
- nystrom_core: bfloat16 [2, 512, 512], replicated, may hold values from -0.5 to 3
Outputs:
- new_coefficients: float32 [32768, 256], P('pts')
- new_momentum: float32 [32768, 256], P('pts')
The draws below stay inside these ranges and needn't reach their ends.
Inputs may be any that keep to these rules, and one draw needn't show every extreme that they name: `block_index`: each row lists 2048 distinct points; a point p belongs to index p // 1024 of pts; in each row one index of pts, drawn from the seed, owns exactly 24 of the points in every aligned group of 256 positions, and no index owns more than 24 points of any such group. `pivot_index`: each row lists 512 distinct positions.
All inputs are finite; a program needn't handle non-finite values.
Results may differ from the reference program's by a relative error of at most 0.0041.
The reference program's roundings to bfloat16 on the way count: a program that leaves them out, or rounds other values in their place, can miss the bound.
Values may be sent and summed in bfloat16 or wider, within the bound.
A program may use at most 64 MiB of HBM per device.

```python
import math
import jax
import jax.numpy as jnp
from jax import lax

DF = 128
NOUT = 256
BLK = 2048
RANK = 512
UPDATES = 2
PTS_DEV = 1024
NPTS = 32768
GROUP = 256
CAP = 24
N_PTS = 32


def shuffle_points(one_key):
    return jax.random.permutation(one_key, PTS_DEV).astype(jnp.int32)


def pick_block(key):
    owner_count = NPTS // PTS_DEV
    group_count = BLK // GROUP
    busy_key, group_key, place_key = jax.random.split(key, 3)
    busiest = jax.random.randint(busy_key, (), 0, owner_count).astype(jnp.int32)
    group_keys = jax.random.split(group_key, group_count)

    def fill_group(group_one):
        ticket_key, order_key = jax.random.split(group_one)
        tickets = jax.random.permutation(ticket_key, (owner_count - 1) * CAP)[:GROUP - CAP].astype(jnp.int32)
        others = (busiest + 1 + tickets // CAP) % owner_count
        sequence = jnp.concatenate([jnp.full((CAP,), busiest, jnp.int32), others.astype(jnp.int32)])
        return jax.random.permutation(order_key, sequence).astype(jnp.int32)
    owner = jax.vmap(fill_group)(group_keys).reshape(BLK).astype(jnp.int32)
    marks = (owner[:, None] == jnp.arange(owner_count, dtype=jnp.int32)[None, :]).astype(jnp.int32)
    before = jnp.cumsum(marks, axis=0) - marks
    rank_within = jnp.sum(before * marks, axis=1).astype(jnp.int32)
    shuffles = jax.vmap(shuffle_points)(jax.random.split(place_key, owner_count))
    return (owner * PTS_DEV + shuffles[owner, rank_within]).astype(jnp.int32)


def draw_block_index(key, part):
    keys = jax.random.split(key, UPDATES)
    return jax.vmap(pick_block)(keys).astype(jnp.int32)


def pick_pivots(key):
    scores = jax.random.randint(key, (BLK,), 0, 32768) * BLK + jnp.arange(BLK, dtype=jnp.int32)
    return lax.top_k(scores.astype(jnp.int32), RANK)[1].astype(jnp.int32)


def draw_pivot_index(key, part):
    keys = jax.random.split(key, UPDATES)
    return jax.vmap(pick_pivots)(keys).astype(jnp.int32)


def draw_nystrom_core(key, part):
    diag_key, off_key = jax.random.split(key, 2)
    diagonal = jax.random.uniform(diag_key, (UPDATES, RANK), jnp.float32, 1.2, 2.8)
    spread = 0.45 / math.sqrt(RANK)
    raw_part = jax.random.normal(off_key, (UPDATES, RANK, RANK), jnp.float32) * spread
    off_part = (raw_part + jnp.swapaxes(raw_part, 1, 2)) * (1.0 / math.sqrt(2.0))
    centred = jnp.eye(RANK, dtype=jnp.float32)[None, :, :] * diagonal[:, :, None]
    centred = centred - (diagonal[:, :, None] + diagonal[:, None, :]) / RANK
    centred = centred + jnp.sum(diagonal, axis=1)[:, None, None] / (RANK * RANK)
    return jnp.clip(centred + off_part, -0.5, 3.0).astype(jnp.bfloat16)


def steps_of(rng, shape, cuts, least, top_value):
    factor_of, own = 1.0, jax.random.fold_in(rng, 6)
    for axis_at, shards_of in cuts:
        heights = jnp.exp(jax.random.uniform(jax.random.fold_in(own, axis_at), (shards_of,), jnp.float32, least / len(cuts), top_value / len(cuts)))
        factor_of = factor_of * jnp.repeat(heights, shape[axis_at] // shards_of).reshape([-1 if axis == axis_at else 1 for axis in range(len(shape))])
    return factor_of


def normal_values(key, extent, deviation, most, shards=(), held_as=jnp.bfloat16):
    entries = deviation * jax.random.normal(key, extent, jnp.float32)
    if shards:
        entries = entries * steps_of(key, extent, shards, -0.22, 0.18)
    return jnp.clip(entries, -most, most).astype(held_as)


def setup_inputs(seed: int = 0) -> dict:
    arg_keys = jax.random.split(jax.random.key(seed), 8)
    return {
        "features": normal_values(arg_keys[0], (NPTS, DF), 1.0, 6.0, ((0, 32),)),
        "targets": normal_values(arg_keys[1], (NPTS, NOUT), 1.0, 6.0, ((0, 32),)),
        "coefficients": normal_values(arg_keys[2], (NPTS, NOUT), 1.0, 6.0, ((0, 32),), jnp.float32),
        "momentum": normal_values(arg_keys[3], (NPTS, NOUT), 1.0, 6.0, ((0, 32),), jnp.float32),
        "block_index": draw_block_index(jax.random.fold_in(arg_keys[7], 71), 0),
        "pivot_index": draw_pivot_index(jax.random.fold_in(arg_keys[7], 71), 0),
        "nystrom_core": draw_nystrom_core(jax.random.fold_in(arg_keys[7], 71), 0),
    }


alpha_mix = 0.6
beta_keep = 0.9
step_size = 0.2
momentum_gain = 1.5
ridge_term = 1.0


def kernel_tile(left_rows, right_rows):
    inner_prod = lax.dot_general(left_rows, right_rows, (((1,), (1,)), ((), ())), preferred_element_type=jnp.float32)
    left_sq = jnp.sum(jnp.square(left_rows.astype(jnp.float32)), axis=1)
    right_sq = jnp.sum(jnp.square(right_rows.astype(jnp.float32)), axis=1)
    squared = left_sq[:, None] + right_sq[None, :] - 2.0 * inner_prod
    return jnp.exp(squared * (-3.5 / left_rows.shape[1])).astype(jnp.bfloat16)


def reference(features, targets, coefficients, momentum, block_index, pivot_index, nystrom_core):
    current = coefficients
    momentum_now = momentum
    feat_blocks = features.reshape(N_PTS, PTS_DEV, DF)
    for update in range(UPDATES):
        mixed = alpha_mix * momentum_now + (1.0 - alpha_mix) * current
        mixed_bf = mixed.astype(jnp.bfloat16)
        block_points = block_index[update]
        block_feats = features[block_points]
        offset = ridge_term * mixed[block_points] - targets[block_points].astype(jnp.float32)

        def accumulate(running, pieces):
            feat_piece, coef_piece = pieces
            return running + jnp.dot(kernel_tile(block_feats, feat_piece), coef_piece, preferred_element_type=jnp.float32), None

        running, unused = lax.scan(accumulate, jnp.zeros((BLK, NOUT), jnp.float32), (feat_blocks, mixed_bf.reshape(N_PTS, PTS_DEV, NOUT)))
        resid = running + offset
        resid_bf = resid.astype(jnp.bfloat16)
        pivot_feats = block_feats[pivot_index[update]]
        factor = kernel_tile(block_feats, pivot_feats)
        proj = lax.dot_general(factor, resid_bf, (((0,), (0,)), ((), ())), preferred_element_type=jnp.float32)
        lifted = jnp.dot(nystrom_core[update], proj.astype(jnp.bfloat16), preferred_element_type=jnp.float32).astype(jnp.bfloat16)
        step_bf = (resid - jnp.dot(factor, lifted, preferred_element_type=jnp.float32)).astype(jnp.bfloat16)
        step_bf = lax.optimization_barrier(step_bf)
        change = step_bf.astype(jnp.float32)
        current = mixed.at[block_points].add(-step_size * change)
        momentum_now = (beta_keep * momentum_now + (1.0 - beta_keep) * mixed).at[block_points].add(-step_size * momentum_gain * change)
    return current, momentum_now
```

```python
import functools

import jax
import jax.numpy as jnp
from jax import lax
from jax.experimental import pallas as pl
from jax.experimental.pallas import tpu as pltpu
from jax.sharding import PartitionSpec as P

alpha_mix = 0.6
beta_keep = 0.9
step_size = 0.2
momentum_gain = 1.5
ridge_term = 1.0

F32 = jnp.float32
BF16 = jnp.bfloat16
NN = (((1,), (0,)), ((), ()))
NT = (((1,), (1,)), ((), ()))
MESH = pl.DeviceIdType.MESH

PTS = 32
ROWS = 8
LOCAL = 1024
GROUP = 256
SLOTS = 32


def dot(left, right, dims=NN):
    return lax.dot_general(left, right, dims, preferred_element_type=F32)


def row_norms(rows):
    squares = jnp.square(rows.astype(F32))
    high = squares.astype(BF16)
    low = (squares - high.astype(F32)).astype(BF16)
    ones = jnp.ones((8, rows.shape[1]), BF16)
    return dot(ones, high, NT) + dot(ones, low, NT)


def kernel_tile(left, right, right_sq):
    scale = -3.5 / left.shape[1]
    left_sq = jnp.sum(jnp.square(left.astype(F32)), axis=1, keepdims=True)
    squared = left_sq + right_sq - 2.0 * dot(left, right, NT)
    return jnp.exp(squared * scale).astype(BF16)


def iota(shape, axis):
    return lax.broadcasted_iota(jnp.int32, shape, axis).astype(F32)


def owner_of(index):
    return jnp.floor(index * (1.0 / LOCAL))


def mod4(value):
    return value - 4.0 * jnp.floor(value * 0.25)


def stack(value):
    return jnp.concatenate([value[:, :128], value[:, 128:]], axis=0)


def unstack(value):
    return [value[:8], value[8:]]


def block_kernel(
    bi_ref, pv_ref, x_ref, w_hbm, z_hbm, t_hbm, core_hbm,
    steps_ref, places_ref,
    idx_ref, idxt_ref, w_ref, z_ref, t_ref, core_ref, load_sem,
    sel_ref, g_snd, g_rcv, feats_ref, factor_ref, cross_ref, mixb_ref, baseb_ref,
    off_ref, baserow_ref, rs0_snd, rs0_rcv, rs1_snd, rs1_rcv, ax_ref, d_snd, d_rcv,
    send_sem, recv_sem,
):
    me_r = lax.axis_index("rows")
    me_p = lax.axis_index("pts")
    core = lax.rem(me_r, 2)
    chip = me_r // 2
    p_f = me_p.astype(F32)
    r_f = me_r.astype(F32)

    barrier = pltpu.get_barrier_semaphore()

    def greet_pts(hop, carry):
        pl.semaphore_signal(
            barrier, inc=1, device_id={"pts": lax.rem(me_p + hop, PTS)}, device_id_type=MESH
        )
        return carry

    def greet_rows(hop, carry):
        pl.semaphore_signal(
            barrier, inc=1, device_id={"rows": lax.rem(me_r + hop, ROWS)}, device_id_type=MESH
        )
        return carry

    lax.fori_loop(1, PTS, greet_pts, 0)
    lax.fori_loop(1, ROWS, greet_rows, 0)

    loads = [
        pltpu.make_async_copy(src, dst, load_sem.at[at])
        for at, (src, dst) in enumerate(
            [(w_hbm, w_ref), (z_hbm, z_ref), (t_hbm, t_ref), (core_hbm, core_ref)]
        )
    ]
    for load in loads:
        load.start()

    def wait_bytes(ref, sem):
        pltpu.make_async_copy(ref, ref, sem).wait()

    idx_ref[...] = jnp.zeros_like(idx_ref)
    for update in range(2):
        for group in range(ROWS):
            at = update * ROWS + group
            idx_ref[at : at + 1, :] = bi_ref[
                update : update + 1, group * GROUP : (group + 1) * GROUP
            ].astype(F32)
        own = pl.ds(pl.multiple_of(me_r * GROUP, GROUP), GROUP)
        idx_ref[16 + update : 17 + update, :] = bi_ref[update : update + 1, own].astype(F32)
        for half in range(2):
            at = 18 + update * 2 + half
            idx_ref[at : at + 1, :] = pv_ref[
                update : update + 1, half * GROUP : (half + 1) * GROUP
            ].astype(F32)
    idxt_ref[...] = jnp.transpose(idx_ref[...])

    below = iota((GROUP, GROUP), 1) < iota((GROUP, GROUP), 0)
    above = iota((GROUP, GROUP), 0) < iota((GROUP, GROUP), 1)
    ones_mat = jnp.ones((GROUP, 128), BF16)

    def owners(at):
        return owner_of(idxt_ref[:, at : at + 1]), owner_of(idx_ref[at : at + 1, :])

    def rank_col(at):
        col, row = owners(at)
        same = jnp.where((col == row) & below, 1.0, 0.0).astype(BF16)
        return dot(same, ones_mat)

    def rank_row(at):
        col, row = owners(at)
        same = jnp.where((col == row) & above, 1.0, 0.0).astype(BF16)
        return dot(jnp.ones((8, GROUP), BF16), same)

    for update in range(2):
        row = idx_ref[16 + update : 17 + update, :]
        rank = rank_row(16 + update)[0:1]
        slot = jnp.where(owner_of(row) == p_f, rank, -1.0)
        pick = jnp.where(iota((SLOTS, GROUP), 0) == slot, 1.0, 0.0).astype(BF16)
        col = idxt_ref[:, 16 + update : 17 + update] - p_f * LOCAL
        hot = jnp.where(iota((GROUP, LOCAL), 1) == col, 1.0, 0.0).astype(BF16)
        place = dot(pick, hot).astype(BF16)
        g_snd[update] = dot(place, x_ref[...]).astype(BF16)

    pl.semaphore_wait(barrier, PTS + ROWS - 2)

    def to_pts(src_of, dst, sem):
        def send(hop, carry):
            peer = lax.rem(me_p + hop, PTS)
            pltpu.make_async_remote_copy(
                src_ref=src_of(peer), dst_ref=dst.at[me_p],
                send_sem=send_sem.at[sem], recv_sem=recv_sem.at[sem],
                device_id={"pts": peer}, device_id_type=MESH,
            ).start()
            return carry

        lax.fori_loop(1, PTS, send, 0)

    def to_rows(buf, sem):
        def send(hop, carry):
            peer = lax.rem(me_r + hop, ROWS)
            pltpu.make_async_remote_copy(
                src_ref=buf.at[me_r], dst_ref=buf.at[me_r],
                send_sem=send_sem.at[sem], recv_sem=recv_sem.at[sem],
                device_id={"rows": peer}, device_id_type=MESH,
            ).start()
            return carry

        lax.fori_loop(1, ROWS, send, 0)

    G, RS0, RS1, AX, DS, FX, FC = 0, 2, 3, 4, 7, 9, 11
    for update in range(2):
        to_pts(lambda peer: g_snd.at[update], g_rcv.at[update], G + update)
        g_rcv[update, me_p] = g_snd[update]

    loads[0].wait()
    loads[1].wait()
    w_now = w_ref[...]
    z_now = z_ref[...]
    mixed = alpha_mix * z_now + (1.0 - alpha_mix) * w_now
    base = alpha_mix * (beta_keep * z_now + (1.0 - beta_keep) * mixed) + (1.0 - alpha_mix) * mixed
    mixb_ref[...] = mixed.astype(BF16)
    baseb_ref[...] = base.astype(BF16)
    loads[2].wait()
    targets = t_ref[...].astype(F32)
    for update, value in enumerate((mixed, base)):
        wanted = ridge_term * value - targets
        high = wanted.astype(BF16)
        low = (wanted - high.astype(F32)).astype(BF16)
        col = idxt_ref[:, 16 + update : 17 + update] - p_f * LOCAL
        hot = jnp.where(iota((GROUP, LOCAL), 1) == col, 1.0, 0.0).astype(BF16)
        off_ref[update] = dot(hot, high) + dot(hot, low)
        if update == 0:
            baserow_ref[...] = dot(hot, baseb_ref[...])

    x_sq = row_norms(x_ref[...])[0:1]

    def select_group(at, group_f, update):
        col = owner_of(idxt_ref[:, at : at + 1])
        quad = jnp.floor(col * 0.25)
        chunk = mod4(col - 4.0 * quad + group_f)
        slot = rank_col(at) + (quad * 128.0 + chunk * SLOTS)
        for block in range(ROWS):
            hit = iota((GROUP, 128), 1) + 128.0 * block == slot
            sel_ref[at, :, block * 128 : (block + 1) * 128] = jnp.where(hit, 1.0, 0.0).astype(BF16)

    for update in range(2):
        for group in range(ROWS):
            select_group(update * ROWS + group, float(group), update)

    my_quad = me_p // 4
    my_kind = p_f - 4.0 * my_quad.astype(F32)
    chunk_of = jnp.floor(iota((8, 128), 1) * (1.0 / SLOTS))
    places_ref[...] = jnp.zeros_like(places_ref)
    for update in range(2):
        for half in range(2):
            total = jnp.zeros((8, 128), F32)
            for part in range(4):
                group = half * 4 + part
                at = update * ROWS + group
                row = idx_ref[at : at + 1, :]
                inner = row - LOCAL * owner_of(row)
                upper = jnp.floor(inner * (1.0 / 32.0))
                lhs = jnp.concatenate(
                    [upper, inner - 32.0 * upper, jnp.ones_like(row), jnp.zeros((5, GROUP), F32)],
                    axis=0,
                ).astype(BF16)
                block = sel_ref[at, :, pl.ds(pl.multiple_of(my_quad * 128, 128), 128)]
                found = dot(lhs, block)
                total = jnp.where(chunk_of == mod4(my_kind + part), found, total)
            point = 32.0 * total[0:1] + total[1:2] - (1.0 - total[2:3])
            places_ref[update : update + 1, half * 128 : (half + 1) * 128] = point

    slots_iota = iota((GROUP, PTS * SLOTS), 1)

    def own_features(update):
        wait_bytes(g_rcv.at[update, pl.ds(0, PTS - 1)], recv_sem.at[G + update])
        col = owner_of(idxt_ref[:, 16 + update : 17 + update])
        slot = rank_col(16 + update)[:, 0:1] + col * SLOTS
        hot = jnp.where(slots_iota == slot, 1.0, 0.0).astype(BF16)
        rows = dot(hot, g_rcv[update].reshape(PTS * SLOTS, 128)).astype(BF16)
        feats_ref[update, core, chip] = rows
        for hop in range(1, 4):
            pltpu.make_async_remote_copy(
                src_ref=feats_ref.at[update, core, chip],
                dst_ref=feats_ref.at[update, core, chip],
                send_sem=send_sem.at[FX + update], recv_sem=recv_sem.at[FX + update],
                device_id={"rows": lax.rem(me_r + 2 * hop, ROWS)}, device_id_type=MESH,
            ).start()
        return rows

    def share_with_core(update):
        wait_bytes(feats_ref.at[update, core, pl.ds(0, 3)], recv_sem.at[FX + update])
        pltpu.make_async_remote_copy(
            src_ref=feats_ref.at[update, core], dst_ref=feats_ref.at[update, core],
            send_sem=send_sem.at[FC + update], recv_sem=recv_sem.at[FC + update],
            device_id={"rows": chip * 2 + 1 - core}, device_id_type=MESH,
        ).start()

    def group_rows(update, group):
        return feats_ref[update, lax.rem(group, 2), group // 2]

    def partial_rows(rows, coefs, offset):
        tile = kernel_tile(rows, x_ref[...], x_sq)
        return dot(tile, coefs) + offset

    def put_pieces(dst, value, lead):
        flipped = jnp.transpose(value)
        for piece in range(PTS):
            dst[piece, lead : lead + 16, :] = stack(
                flipped[piece * 8 : piece * 8 + 8]
            ).astype(BF16)

    rows0 = own_features(0)
    put_pieces(rs0_snd, partial_rows(rows0, mixb_ref[...], off_ref[0]), 0)
    to_pts(lambda peer: rs0_snd.at[peer], rs0_rcv, RS0)
    rs0_rcv[me_p] = rs0_snd[me_p]

    rows1 = own_features(1)
    put_pieces(rs1_snd, partial_rows(rows1, baseb_ref[...], off_ref[1]), 0)
    put_pieces(rs1_snd, baserow_ref[...], 16)
    to_pts(lambda peer: rs1_snd.at[peer], rs1_rcv, RS1)
    rs1_rcv[me_p] = rs1_snd[me_p]

    def make_factor(update):
        share_with_core(update)
        wait_bytes(feats_ref.at[update, core], recv_sem.at[FC + update])
        pivots = []
        for half in range(2):
            at = 18 + update * 2 + half
            col = idxt_ref[:, at : at + 1]
            total = jnp.zeros((GROUP, 128), F32)
            for group in range(ROWS):
                hot = jnp.where(iota((GROUP, GROUP), 1) + float(group * GROUP) == col, 1.0, 0.0)
                total = total + dot(hot.astype(BF16), feats_ref[update, group % 2, group // 2])
            pivots.append(total.astype(BF16))
        pivots = jnp.concatenate(pivots, axis=0)
        pivots_sq = row_norms(pivots)[0:1]

        def body(group, carry):
            at = pl.ds(pl.multiple_of(group * GROUP, GROUP), GROUP)
            factor_ref[update, at, :] = kernel_tile(group_rows(update, group), pivots, pivots_sq)
            return carry

        lax.fori_loop(0, ROWS, body, 0)

    make_factor(0)
    rows1_sq = row_norms(rows1)[0:1]
    row1 = idx_ref[17:18, :]
    for group in range(ROWS):
        tile = kernel_tile(feats_ref[0, group % 2, group // 2], rows1, rows1_sq)
        same = jnp.where(idxt_ref[:, group : group + 1] == row1, ridge_term, 0.0)
        cross_ref[group * GROUP : (group + 1) * GROUP, :] = (tile.astype(F32) + same).astype(BF16)

    def sum_pieces(rcv, lead):
        total = rcv[0, lead : lead + 16, :].astype(F32)
        for piece in range(1, PTS):
            total = total + rcv[piece, lead : lead + 16, :].astype(F32)
        return total

    def share_rows(at, value):
        ax_ref[at, me_r] = value.astype(BF16)
        to_rows(ax_ref.at[at], AX + at)

    def whole_rows(at):
        wait_bytes(ax_ref.at[at, pl.ds(0, ROWS - 1)], recv_sem.at[AX + at])
        parts = []
        for group in range(ROWS):
            parts += unstack(ax_ref[at, group].astype(F32))
        return jnp.concatenate(parts, axis=1)

    wait_bytes(rs0_rcv.at[pl.ds(0, PTS - 1)], recv_sem.at[RS0])
    share_rows(0, sum_pieces(rs0_rcv, 0))
    wait_bytes(rs1_rcv.at[pl.ds(0, PTS - 1)], recv_sem.at[RS1])
    share_rows(1, sum_pieces(rs1_rcv, 16))
    partial1 = sum_pieces(rs1_rcv, 0)
    make_factor(1)
    loads[3].wait()

    def step_of(update, resid):
        proj = dot(resid.astype(BF16), factor_ref[update])
        lifted = dot(proj.astype(BF16), core_ref[update], NT).astype(BF16)
        return (resid - dot(lifted, factor_ref[update], NT)).astype(BF16)

    def send_steps(update, step):
        chunk_at = jnp.floor(iota((8, 128), 1) * (1.0 / SLOTS))
        for half in range(2):
            found = []
            for part in range(4):
                group = half * 4 + part
                found.append(
                    dot(step[:, group * GROUP : (group + 1) * GROUP], sel_ref[update * ROWS + group])
                )
            for owner in range(PTS):
                block = owner // 4
                kind = owner % 4
                total = jnp.zeros((8, 128), F32)
                for part in range(4):
                    piece = found[part][:, block * 128 : (block + 1) * 128]
                    total = jnp.where(chunk_at == float((kind + part) % 4), piece, total)
                d_snd[update, owner, half] = total
        for owner in range(PTS):
            d_out = jnp.concatenate([d_snd[update, owner, 0], d_snd[update, owner, 1]], axis=0)
            d_rcv[2 + update, owner] = d_out.astype(BF16)
        to_pts(lambda peer: d_rcv.at[2 + update, peer], d_rcv.at[update], DS + update)
        d_rcv[update, me_p] = d_rcv[2 + update, me_p]

    resid0 = whole_rows(0)
    step0 = step_of(0, resid0)
    base_rows = whole_rows(1)
    drop = alpha_mix * step_size * momentum_gain + (1.0 - alpha_mix) * step_size
    moved = (base_rows - drop * step0.astype(F32)).astype(BF16).astype(F32) - base_rows
    high = moved.astype(BF16)
    low = (moved - high.astype(F32)).astype(BF16)
    lhs = jnp.concatenate([high.astype(F32), low.astype(F32)], axis=0).astype(BF16)
    change = dot(lhs, cross_ref[...])
    share_rows(2, partial1 + stack(change[:8] + change[8:]))
    send_steps(0, step0)
    step1 = step_of(1, whole_rows(2))
    send_steps(1, step1)

    for update in range(2):
        wait_bytes(d_rcv.at[update, pl.ds(0, PTS - 1)], recv_sem.at[DS + update])
        steps_ref[update] = d_rcv[update]

    for update in range(2):
        wait_bytes(g_rcv.at[update, pl.ds(0, PTS - 1)], send_sem.at[G + update])
        wait_bytes(feats_ref.at[update, core, pl.ds(0, 3)], send_sem.at[FX + update])
        wait_bytes(feats_ref.at[update, core], send_sem.at[FC + update])
        wait_bytes(d_rcv.at[update, pl.ds(0, PTS - 1)], send_sem.at[DS + update])
    wait_bytes(rs0_rcv.at[pl.ds(0, PTS - 1)], send_sem.at[RS0])
    wait_bytes(rs1_rcv.at[pl.ds(0, PTS - 1)], send_sem.at[RS1])
    for at in range(3):
        wait_bytes(ax_ref.at[at, pl.ds(0, ROWS - 1)], send_sem.at[AX + at])


def apply_kernel(w_ref, z_ref, steps_ref, places_ref, w_out, z_out):
    rows = w_ref.shape[0]
    first = (pl.program_id(0) * rows).astype(F32)

    def change(update):
        halves = []
        for half in range(2):
            cut = slice(half * 8, half * 8 + 8)
            halves.append(
                jnp.concatenate(
                    [steps_ref[update, piece].astype(F32)[cut] for piece in range(PTS)], axis=0
                )
            )
        steps = jnp.concatenate(halves, axis=1).astype(BF16)
        place = places_ref[update : update + 1, :]
        hot = jnp.where(iota((rows, GROUP), 0) + first == place, 1.0, 0.0).astype(BF16)
        return dot(hot, steps, NT)

    current = w_ref[...]
    momentum_now = z_ref[...]
    for update in range(2):
        delta = change(update)
        mixed = alpha_mix * momentum_now + (1.0 - alpha_mix) * current
        current = mixed - step_size * delta
        momentum_now = (
            beta_keep * momentum_now + (1.0 - beta_keep) * mixed
        ) - step_size * momentum_gain * delta
    w_out[...] = current
    z_out[...] = momentum_now


def shards(features, targets, coefficients, momentum, block_index, pivot_index, nystrom_core):
    vmem = pl.BlockSpec(memory_space=pltpu.VMEM)
    anywhere = pl.BlockSpec(memory_space=pl.ANY)
    steps, places = pl.pallas_call(
        block_kernel,
        out_shape=(
            jax.ShapeDtypeStruct((2, PTS, 16, 128), BF16),
            jax.ShapeDtypeStruct((8, GROUP), F32),
        ),
        in_specs=[vmem, vmem, vmem, anywhere, anywhere, anywhere, anywhere],
        out_specs=(vmem, vmem),
        scratch_shapes=[
            pltpu.VMEM((128, GROUP), F32),
            pltpu.VMEM((GROUP, 128), F32),
            pltpu.VMEM((LOCAL, 256), F32),
            pltpu.VMEM((LOCAL, 256), F32),
            pltpu.VMEM((LOCAL, 256), BF16),
            pltpu.VMEM((2, 512, 512), BF16),
            pltpu.SemaphoreType.DMA((4,)),
            pltpu.VMEM((16, GROUP, PTS * SLOTS), BF16),
            pltpu.VMEM((2, SLOTS, 128), BF16),
            pltpu.VMEM((2, PTS, SLOTS, 128), BF16),
            pltpu.VMEM((2, 2, 4, GROUP, 128), BF16),
            pltpu.VMEM((2, ROWS * GROUP, 512), BF16),
            pltpu.VMEM((ROWS * GROUP, GROUP), BF16),
            pltpu.VMEM((LOCAL, 256), BF16),
            pltpu.VMEM((LOCAL, 256), BF16),
            pltpu.VMEM((2, GROUP, 256), F32),
            pltpu.VMEM((GROUP, 256), F32),
            pltpu.VMEM((PTS, 16, 128), BF16),
            pltpu.VMEM((PTS, 16, 128), BF16),
            pltpu.VMEM((PTS, 32, 128), BF16),
            pltpu.VMEM((PTS, 32, 128), BF16),
            pltpu.VMEM((3, ROWS, 16, 128), BF16),
            pltpu.VMEM((2, PTS, 2, 8, 128), F32),
            pltpu.VMEM((4, PTS, 16, 128), BF16),
            pltpu.SemaphoreType.DMA((13,)),
            pltpu.SemaphoreType.DMA((13,)),
        ],
        compiler_params=pltpu.CompilerParams(
            collective_id=0, has_side_effects=True, vmem_limit_bytes=56 * 1024 * 1024
        ),
        name="block_steps",
    )(block_index, pivot_index, features, coefficients, momentum, targets, nystrom_core)

    tile = 256
    by_rows = pl.BlockSpec((tile, 256), lambda at: (at, 0))
    return pl.pallas_call(
        apply_kernel,
        grid=(LOCAL // tile,),
        out_shape=(
            jax.ShapeDtypeStruct(coefficients.shape, F32),
            jax.ShapeDtypeStruct(momentum.shape, F32),
        ),
        in_specs=[
            by_rows,
            by_rows,
            pl.BlockSpec((2, PTS, 16, 128), lambda at: (0, 0, 0, 0)),
            pl.BlockSpec((8, GROUP), lambda at: (0, 0)),
        ],
        out_specs=(by_rows, by_rows),
        name="apply_steps",
    )(coefficients, momentum, steps, places)


def solution(mesh):
    in_specs = (P("pts", None), P("pts", None), P("pts", None), P("pts", None), P(), P(), P())
    out_specs = (P("pts", None), P("pts", None))
    return jax.shard_map(shards, mesh=mesh, in_specs=in_specs, out_specs=out_specs, check_vma=False)
```

```python
import functools

import jax
import jax.numpy as jnp
from jax import lax
from jax.experimental import pallas as pl
from jax.experimental.pallas import tpu as pltpu
from jax.sharding import PartitionSpec as P

alpha_mix = 0.6
beta_keep = 0.9
step_size = 0.2
momentum_gain = 1.5
ridge_term = 1.0

F32 = jnp.float32
BF16 = jnp.bfloat16
NN = (((1,), (0,)), ((), ()))
NT = (((1,), (1,)), ((), ()))
MESH = pl.DeviceIdType.MESH

PTS = 32
ROWS = 8
LOCAL = 1024
GROUP = 256
CAP = 24
SLOTS = 32


def dot(left, right, dims=NN):
    return lax.dot_general(left, right, dims, preferred_element_type=F32)


def row_norms(rows):
    squares = jnp.square(rows.astype(F32))
    high = squares.astype(BF16)
    low = (squares - high.astype(F32)).astype(BF16)
    ones = jnp.ones((8, rows.shape[1]), BF16)
    return dot(ones, high, NT) + dot(ones, low, NT)


def kernel_tile(left, right, right_sq):
    scale = -3.5 / left.shape[1]
    left_sq = jnp.sum(jnp.square(left.astype(F32)), axis=1, keepdims=True)
    squared = left_sq + right_sq - 2.0 * dot(left, right, NT)
    return jnp.exp(squared * scale).astype(BF16)


def iota(shape, axis):
    return lax.broadcasted_iota(jnp.int32, shape, axis).astype(F32)


def owner_of(index):
    return jnp.floor(index * (1.0 / LOCAL))


def mod4(value):
    return value - 4.0 * jnp.floor(value * 0.25)


def stack(value):
    return jnp.concatenate([value[:, :128], value[:, 128:]], axis=0)


def unstack(value):
    return [value[:8], value[8:]]


def apply_update(current, momentum_now, steps, place, first):
    hot = jnp.where(iota((current.shape[0], GROUP), 0) + first == place, 1.0, 0.0).astype(BF16)
    delta = dot(hot, steps, NT)
    mixed = alpha_mix * momentum_now + (1.0 - alpha_mix) * current
    current = mixed - step_size * delta
    momentum_now = (
        beta_keep * momentum_now + (1.0 - beta_keep) * mixed
    ) - step_size * momentum_gain * delta
    return current, momentum_now


def block_kernel(
    bi_ref, pv_ref, x_ref, w_hbm, z_hbm, t_hbm, core_hbm,
    w_mid, z_mid, steps_ref, places_ref,
    idx_ref, idxt_ref, w_ref, z_ref, t_ref, core_ref, load_sem,
    sel_ref, g_snd, g_rcv, feats_ref, factor_ref, cross_ref, mixb_ref, baseb_ref,
    off_ref, rs0_snd, rs0_rcv, rs1_snd, rs1_rcv, ax_ref, d_snd, d_rcv,
    send_sem, recv_sem,
):
    me_r = lax.axis_index("rows")
    me_p = lax.axis_index("pts")
    core = lax.rem(me_r, 2)
    chip = me_r // 2
    p_f = me_p.astype(F32)
    r_f = me_r.astype(F32)

    barrier = pltpu.get_barrier_semaphore()

    def greet_pts(hop, carry):
        pl.semaphore_signal(
            barrier, inc=1, device_id={"pts": lax.rem(me_p + hop, PTS)}, device_id_type=MESH
        )
        return carry

    def greet_rows(hop, carry):
        pl.semaphore_signal(
            barrier, inc=1, device_id={"rows": lax.rem(me_r + hop, ROWS)}, device_id_type=MESH
        )
        return carry

    lax.fori_loop(1, PTS, greet_pts, 0)
    lax.fori_loop(1, ROWS, greet_rows, 0)

    loads = [
        pltpu.make_async_copy(src, dst, load_sem.at[at])
        for at, (src, dst) in enumerate(
            [(w_hbm, w_ref), (z_hbm, z_ref), (t_hbm, t_ref), (core_hbm, core_ref)]
        )
    ]
    for load in loads:
        load.start()

    def wait_bytes(ref, sem):
        pltpu.make_async_copy(ref, ref, sem).wait()

    arrivals = {}
    sent = []

    def expect(sem, ref):
        arrivals[sem] = ref
        sent.append((sem, ref))

    def arrive(sem):
        wait_bytes(arrivals.pop(sem), recv_sem.at[sem])

    idx_ref[...] = jnp.zeros_like(idx_ref)
    for update in range(2):
        for group in range(ROWS):
            at = update * ROWS + group
            idx_ref[at : at + 1, :] = bi_ref[
                update : update + 1, group * GROUP : (group + 1) * GROUP
            ].astype(F32)
        own = pl.ds(pl.multiple_of(me_r * GROUP, GROUP), GROUP)
        idx_ref[16 + update : 17 + update, :] = bi_ref[update : update + 1, own].astype(F32)
        for half in range(2):
            at = 18 + update * 2 + half
            idx_ref[at : at + 1, :] = pv_ref[
                update : update + 1, half * GROUP : (half + 1) * GROUP
            ].astype(F32)
    idxt_ref[...] = jnp.transpose(idx_ref[...])

    below = iota((GROUP, GROUP), 1) < iota((GROUP, GROUP), 0)
    above = iota((GROUP, GROUP), 0) < iota((GROUP, GROUP), 1)
    ones_mat = jnp.ones((GROUP, 128), BF16)

    def owners(at):
        return owner_of(idxt_ref[:, at : at + 1]), owner_of(idx_ref[at : at + 1, :])

    def rank_col(at):
        col, row = owners(at)
        same = jnp.where((col == row) & below, 1.0, 0.0).astype(BF16)
        return dot(same, ones_mat)

    def rank_row(at):
        col, row = owners(at)
        same = jnp.where((col == row) & above, 1.0, 0.0).astype(BF16)
        return dot(jnp.ones((8, GROUP), BF16), same)

    for update in range(2):
        row = idx_ref[16 + update : 17 + update, :]
        rank = rank_row(16 + update)[0:1]
        slot = jnp.where(owner_of(row) == p_f, rank, -1.0)
        pick = jnp.where(iota((CAP, GROUP), 0) == slot, 1.0, 0.0).astype(BF16)
        col = idxt_ref[:, 16 + update : 17 + update] - p_f * LOCAL
        hot = jnp.where(iota((GROUP, LOCAL), 1) == col, 1.0, 0.0).astype(BF16)
        place = dot(pick, hot).astype(BF16)
        g_snd[update] = dot(place, x_ref[...]).astype(BF16)

    pl.semaphore_wait(barrier, PTS + ROWS - 2)

    def to_pts(src_of, dst, sem):
        def send(hop, carry):
            peer = lax.rem(me_p + hop, PTS)
            pltpu.make_async_remote_copy(
                src_ref=src_of(peer), dst_ref=dst.at[me_p],
                send_sem=send_sem.at[sem], recv_sem=recv_sem.at[sem],
                device_id={"pts": peer}, device_id_type=MESH,
            ).start()
            return carry

        lax.fori_loop(1, PTS, send, 0)
        expect(sem, dst.at[pl.ds(0, PTS - 1)])

    def to_rows(buf, sem):
        def send(hop, carry):
            peer = lax.rem(me_r + hop, ROWS)
            pltpu.make_async_remote_copy(
                src_ref=buf.at[me_r], dst_ref=buf.at[me_r],
                send_sem=send_sem.at[sem], recv_sem=recv_sem.at[sem],
                device_id={"rows": peer}, device_id_type=MESH,
            ).start()
            return carry

        lax.fori_loop(1, ROWS, send, 0)
        expect(sem, buf.at[pl.ds(0, ROWS - 1)])

    G, RS0, RS1, AX, DS, FX, FC = 0, 2, 3, 4, 6, 8, 10
    for update in range(2):
        to_pts(lambda peer: g_snd.at[update], g_rcv.at[update], G + update)
        g_rcv[update, me_p] = g_snd[update]

    loads[0].wait()
    loads[1].wait()
    w_now = w_ref[...]
    z_now = z_ref[...]
    mixed = alpha_mix * z_now + (1.0 - alpha_mix) * w_now
    base = alpha_mix * (beta_keep * z_now + (1.0 - beta_keep) * mixed) + (1.0 - alpha_mix) * mixed
    mixb_ref[...] = mixed.astype(BF16)
    baseb_ref[...] = base.astype(BF16)
    loads[2].wait()
    targets = t_ref[...].astype(F32)
    for update, value in enumerate((mixed, base)):
        wanted = ridge_term * value - targets
        high = wanted.astype(BF16)
        low = (wanted - high.astype(F32)).astype(BF16)
        col = idxt_ref[:, 16 + update : 17 + update] - p_f * LOCAL
        hot = jnp.where(iota((GROUP, LOCAL), 1) == col, 1.0, 0.0).astype(BF16)
        off_ref[update] = dot(hot, high) + dot(hot, low)

    x_sq = row_norms(x_ref[...])[0:1]

    def select_group(at, group_f, update):
        col = owner_of(idxt_ref[:, at : at + 1])
        quad = jnp.floor(col * 0.25)
        chunk = mod4(col - 4.0 * quad + group_f)
        slot = rank_col(at) + (quad * 128.0 + chunk * SLOTS)
        for block in range(ROWS):
            hit = iota((GROUP, 128), 1) + 128.0 * block == slot
            sel_ref[at, :, block * 128 : (block + 1) * 128] = jnp.where(hit, 1.0, 0.0).astype(BF16)

    for update in range(2):
        for group in range(ROWS):
            select_group(update * ROWS + group, float(group), update)

    my_quad = me_p // 4
    my_kind = p_f - 4.0 * my_quad.astype(F32)
    chunk_of = jnp.floor(iota((8, 128), 1) * (1.0 / SLOTS))
    places_ref[...] = jnp.zeros_like(places_ref)
    for update in range(2):
        for half in range(2):
            total = jnp.zeros((8, 128), F32)
            for part in range(4):
                group = half * 4 + part
                at = update * ROWS + group
                row = idx_ref[at : at + 1, :]
                inner = row - LOCAL * owner_of(row)
                upper = jnp.floor(inner * (1.0 / 32.0))
                lhs = jnp.concatenate(
                    [upper, inner - 32.0 * upper, jnp.ones_like(row), jnp.zeros((5, GROUP), F32)],
                    axis=0,
                ).astype(BF16)
                block = sel_ref[at, :, pl.ds(pl.multiple_of(my_quad * 128, 128), 128)]
                found = dot(lhs, block)
                total = jnp.where(chunk_of == mod4(my_kind + part), found, total)
            point = 32.0 * total[0:1] + total[1:2] - (1.0 - total[2:3])
            places_ref[update : update + 1, half * 128 : (half + 1) * 128] = point

    slots_iota = iota((GROUP, PTS * CAP), 1)

    def own_features(update):
        arrive(G + update)
        col = owner_of(idxt_ref[:, 16 + update : 17 + update])
        slot = rank_col(16 + update)[:, 0:1] + col * CAP
        hot = jnp.where(slots_iota == slot, 1.0, 0.0).astype(BF16)
        rows = dot(hot, g_rcv[update].reshape(PTS * CAP, 128)).astype(BF16)
        feats_ref[update, core, chip] = rows
        for hop in range(1, 4):
            pltpu.make_async_remote_copy(
                src_ref=feats_ref.at[update, core, chip],
                dst_ref=feats_ref.at[update, core, chip],
                send_sem=send_sem.at[FX + update], recv_sem=recv_sem.at[FX + update],
                device_id={"rows": lax.rem(me_r + 2 * hop, ROWS)}, device_id_type=MESH,
            ).start()
        expect(FX + update, feats_ref.at[update, core, pl.ds(0, 3)])
        return rows

    def share_with_core(update):
        arrive(FX + update)
        pltpu.make_async_remote_copy(
            src_ref=feats_ref.at[update, core], dst_ref=feats_ref.at[update, core],
            send_sem=send_sem.at[FC + update], recv_sem=recv_sem.at[FC + update],
            device_id={"rows": chip * 2 + 1 - core}, device_id_type=MESH,
        ).start()
        expect(FC + update, feats_ref.at[update, core])

    def group_rows(update, group):
        return feats_ref[update, lax.rem(group, 2), group // 2]

    def partial_rows(rows, coefs, offset):
        tile = kernel_tile(rows, x_ref[...], x_sq)
        return dot(tile, coefs) + offset

    def put_pieces(dst, value):
        flipped = jnp.transpose(value)
        for piece in range(PTS):
            dst[piece] = stack(flipped[piece * 8 : piece * 8 + 8]).astype(BF16)

    rows0 = own_features(0)
    put_pieces(rs0_snd, partial_rows(rows0, mixb_ref[...], off_ref[0]))
    to_pts(lambda peer: rs0_snd.at[peer], rs0_rcv, RS0)
    rs0_rcv[me_p] = rs0_snd[me_p]

    rows1 = own_features(1)
    put_pieces(rs1_snd, partial_rows(rows1, baseb_ref[...], off_ref[1]))
    to_pts(lambda peer: rs1_snd.at[peer], rs1_rcv, RS1)
    rs1_rcv[me_p] = rs1_snd[me_p]

    def make_factor(update):
        arrive(FC + update)
        pivots = []
        for half in range(2):
            at = 18 + update * 2 + half
            col = idxt_ref[:, at : at + 1]
            total = jnp.zeros((GROUP, 128), F32)
            for group in range(ROWS):
                hot = jnp.where(iota((GROUP, GROUP), 1) + float(group * GROUP) == col, 1.0, 0.0)
                total = total + dot(hot.astype(BF16), feats_ref[update, group % 2, group // 2])
            pivots.append(total.astype(BF16))
        pivots = jnp.concatenate(pivots, axis=0)
        pivots_sq = row_norms(pivots)[0:1]

        def body(group, carry):
            at = pl.ds(pl.multiple_of(group * GROUP, GROUP), GROUP)
            factor_ref[update, at, :] = kernel_tile(group_rows(update, group), pivots, pivots_sq)
            return carry

        lax.fori_loop(0, ROWS, body, 0)

    def sum_pieces(rcv):
        total = rcv[0].astype(F32)
        for piece in range(1, PTS):
            total = total + rcv[piece].astype(F32)
        return total

    def share_rows(at, value):
        ax_ref[at, me_r] = value.astype(BF16)
        to_rows(ax_ref.at[at], AX + at)

    def whole_rows(at):
        arrive(AX + at)
        parts = []
        for group in range(ROWS):
            parts += unstack(ax_ref[at, group].astype(F32))
        return jnp.concatenate(parts, axis=1)

    share_with_core(0)
    arrive(RS0)
    share_rows(0, sum_pieces(rs0_rcv))
    make_factor(0)
    share_with_core(1)
    rows1_sq = row_norms(rows1)[0:1]
    row1 = idx_ref[17:18, :]
    for group in range(ROWS):
        tile = kernel_tile(feats_ref[0, group % 2, group // 2], rows1, rows1_sq)
        same = jnp.where(idxt_ref[:, group : group + 1] == row1, ridge_term, 0.0)
        cross_ref[group * GROUP : (group + 1) * GROUP, :] = (tile.astype(F32) + same).astype(BF16)
    loads[3].wait()

    def step_of(update, resid):
        proj = dot(resid.astype(BF16), factor_ref[update])
        lifted = dot(proj.astype(BF16), core_ref[update], NT).astype(BF16)
        return (resid - dot(lifted, factor_ref[update], NT)).astype(BF16)

    def send_steps(update, step):
        chunk_at = jnp.floor(iota((8, 128), 1) * (1.0 / SLOTS))
        for pair in range(4):
            cut = slice(pair * 256, pair * 256 + 256)
            found = [
                dot(
                    step[:, group * GROUP : (group + 1) * GROUP],
                    sel_ref[update * ROWS + group, :, cut],
                )
                for group in range(ROWS)
            ]
            for at in range(8):
                owner = pair * 8 + at
                halves = []
                for half in range(2):
                    total = jnp.zeros((8, 128), F32)
                    for part in range(4):
                        lanes = slice(at // 4 * 128, at // 4 * 128 + 128)
                        piece = found[half * 4 + part][:, lanes]
                        total = jnp.where(chunk_at == float((owner + part) % 4), piece, total)
                    halves.append(total)
                d_snd[update, owner] = jnp.concatenate(halves, axis=0).astype(BF16)
        to_pts(lambda peer: d_snd.at[update, peer], d_rcv.at[update], DS + update)
        d_rcv[update, me_p] = d_snd[update, me_p]

    def received(update):
        arrive(DS + update)
        halves = []
        for half in range(2):
            cut = slice(half * 8, half * 8 + 8)
            halves.append(
                jnp.concatenate(
                    [d_rcv[update, piece].astype(F32)[cut] for piece in range(PTS)], axis=0
                )
            )
        return jnp.concatenate(halves, axis=1).astype(BF16)

    step0 = step_of(0, whole_rows(0))
    drop = alpha_mix * step_size * momentum_gain + (1.0 - alpha_mix) * step_size
    change = dot(step0, cross_ref[...]) * drop
    arrive(RS1)
    share_rows(1, sum_pieces(rs1_rcv) - stack(change))
    send_steps(0, step0)
    make_factor(1)
    step1 = step_of(1, whole_rows(1))
    send_steps(1, step1)

    steps0 = received(0)
    for part in range(4):
        cut = slice(part * 256, part * 256 + 256)
        current, momentum_now = apply_update(
            w_ref[cut, :], z_ref[cut, :], steps0, places_ref[0:1, :], part * 256.0
        )
        w_ref[cut, :] = current
        z_ref[cut, :] = momentum_now
    stores = [
        pltpu.make_async_copy(src, dst, load_sem.at[at])
        for at, (src, dst) in enumerate([(w_ref, w_mid), (z_ref, z_mid)])
    ]
    for store in stores:
        store.start()
    steps_ref[...] = received(1)

    for store in stores:
        store.wait()
    for sem, ref in sent:
        wait_bytes(ref, send_sem.at[sem])


def apply_kernel(w_ref, z_ref, steps_ref, places_ref, w_out, z_out):
    first = (pl.program_id(0) * w_ref.shape[0]).astype(F32)
    current, momentum_now = apply_update(
        w_ref[...], z_ref[...], steps_ref[...], places_ref[1:2, :], first
    )
    w_out[...] = current
    z_out[...] = momentum_now


def shards(features, targets, coefficients, momentum, block_index, pivot_index, nystrom_core):
    vmem = pl.BlockSpec(memory_space=pltpu.VMEM)
    anywhere = pl.BlockSpec(memory_space=pl.ANY)
    w_mid, z_mid, steps, places = pl.pallas_call(
        block_kernel,
        out_shape=(
            jax.ShapeDtypeStruct(coefficients.shape, F32),
            jax.ShapeDtypeStruct(momentum.shape, F32),
            jax.ShapeDtypeStruct((256, GROUP), BF16),
            jax.ShapeDtypeStruct((8, GROUP), F32),
        ),
        in_specs=[vmem, vmem, vmem, anywhere, anywhere, anywhere, anywhere],
        out_specs=(anywhere, anywhere, vmem, vmem),
        scratch_shapes=[
            pltpu.VMEM((128, GROUP), F32),
            pltpu.VMEM((GROUP, 128), F32),
            pltpu.VMEM((LOCAL, 256), F32),
            pltpu.VMEM((LOCAL, 256), F32),
            pltpu.VMEM((LOCAL, 256), BF16),
            pltpu.VMEM((2, 512, 512), BF16),
            pltpu.SemaphoreType.DMA((4,)),
            pltpu.VMEM((16, GROUP, PTS * SLOTS), BF16),
            pltpu.VMEM((2, CAP, 128), BF16),
            pltpu.VMEM((2, PTS, CAP, 128), BF16),
            pltpu.VMEM((2, 2, 4, GROUP, 128), BF16),
            pltpu.VMEM((2, ROWS * GROUP, 512), BF16),
            pltpu.VMEM((ROWS * GROUP, GROUP), BF16),
            pltpu.VMEM((LOCAL, 256), BF16),
            pltpu.VMEM((LOCAL, 256), BF16),
            pltpu.VMEM((2, GROUP, 256), F32),
            pltpu.VMEM((PTS, 16, 128), BF16),
            pltpu.VMEM((PTS, 16, 128), BF16),
            pltpu.VMEM((PTS, 16, 128), BF16),
            pltpu.VMEM((PTS, 16, 128), BF16),
            pltpu.VMEM((2, ROWS, 16, 128), BF16),
            pltpu.VMEM((2, PTS, 16, 128), BF16),
            pltpu.VMEM((2, PTS, 16, 128), BF16),
            pltpu.SemaphoreType.DMA((12,)),
            pltpu.SemaphoreType.DMA((12,)),
        ],
        compiler_params=pltpu.CompilerParams(
            collective_id=0, has_side_effects=True, vmem_limit_bytes=56 * 1024 * 1024
        ),
        name="block_steps",
    )(block_index, pivot_index, features, coefficients, momentum, targets, nystrom_core)

    tile = 256
    by_rows = pl.BlockSpec((tile, 256), lambda at: (at, 0))
    return pl.pallas_call(
        apply_kernel,
        grid=(LOCAL // tile,),
        out_shape=(
            jax.ShapeDtypeStruct(coefficients.shape, F32),
            jax.ShapeDtypeStruct(momentum.shape, F32),
        ),
        in_specs=[
            by_rows,
            by_rows,
            pl.BlockSpec((256, GROUP), lambda at: (0, 0)),
            pl.BlockSpec((8, GROUP), lambda at: (0, 0)),
        ],
        out_specs=(by_rows, by_rows),
        name="apply_steps",
    )(w_mid, z_mid, steps, places)


def solution(mesh):
    in_specs = (P("pts", None), P("pts", None), P("pts", None), P("pts", None), P(), P(), P())
    out_specs = (P("pts", None), P("pts", None))
    return jax.shard_map(shards, mesh=mesh, in_specs=in_specs, out_specs=out_specs, check_vma=False)
```

```python
import functools

import jax
import jax.numpy as jnp
from jax import lax
from jax.experimental import pallas as pl
from jax.experimental.pallas import tpu as pltpu
from jax.sharding import PartitionSpec as P

alpha_mix = 0.6
beta_keep = 0.9
step_size = 0.2
momentum_gain = 1.5
ridge_term = 1.0

F32 = jnp.float32
BF16 = jnp.bfloat16
NN = (((1,), (0,)), ((), ()))
NT = (((1,), (1,)), ((), ()))
MESH = pl.DeviceIdType.MESH

PTS = 32
ROWS = 8
LOCAL = 1024
GROUP = 256
CAP = 24
VMEM_BYTES = 64_500_000
STORES = 2
SLOTS = 32


def dot(left, right, dims=NN):
    return lax.dot_general(left, right, dims, preferred_element_type=F32)


def row_norms(rows):
    squares = jnp.square(rows.astype(F32))
    high = squares.astype(BF16)
    low = (squares - high.astype(F32)).astype(BF16)
    ones = jnp.ones((8, rows.shape[1]), BF16)
    return dot(ones, high, NT) + dot(ones, low, NT)


def kernel_tile(left, right, right_sq):
    scale = -3.5 / left.shape[1]
    left_sq = jnp.sum(jnp.square(left.astype(F32)), axis=1, keepdims=True)
    squared = left_sq + right_sq - 2.0 * dot(left, right, NT)
    return jnp.exp(squared * scale).astype(BF16)


def iota(shape, axis):
    return lax.broadcasted_iota(jnp.int32, shape, axis).astype(F32)


def owner_of(index):
    return jnp.floor(index * (1.0 / LOCAL))


def mod4(value):
    return value - 4.0 * jnp.floor(value * 0.25)


def stack(value):
    return jnp.concatenate([value[:, :128], value[:, 128:]], axis=0)


def unstack(value):
    return [value[:8], value[8:]]


def apply_update(current, momentum_now, steps, place, first):
    hot = jnp.where(iota((current.shape[0], GROUP), 0) + first == place, 1.0, 0.0).astype(BF16)
    delta = dot(hot, steps, NT)
    mixed = alpha_mix * momentum_now + (1.0 - alpha_mix) * current
    current = mixed - step_size * delta
    momentum_now = (
        beta_keep * momentum_now + (1.0 - beta_keep) * mixed
    ) - step_size * momentum_gain * delta
    return current, momentum_now


def block_kernel(
    bi_ref, pv_ref, x_ref, w_hbm, z_hbm, t_hbm, core_hbm,
    w_mid, z_mid, steps_ref, places_ref,
    idx_ref, idxt_ref, w_ref, z_ref, t_ref, core_ref, load_sem,
    sel_ref, own_sel_ref, pivot_sel_ref, g_snd, g_rcv, feats_ref, factor_ref, cross_ref, mixb_ref, baseb_ref,
    off_ref, rs0_snd, rs0_rcv, rs1_snd, rs1_rcv, ax_ref, d_snd, d_rcv,
    send_sem, recv_sem,
):
    me_r = lax.axis_index("rows")
    me_p = lax.axis_index("pts")
    core = lax.rem(me_r, 2)
    chip = me_r // 2
    p_f = me_p.astype(F32)
    r_f = me_r.astype(F32)

    barrier = pltpu.get_barrier_semaphore()

    def greet_pts(hop, carry):
        pl.semaphore_signal(
            barrier, inc=1, device_id={"pts": lax.rem(me_p + hop, PTS)}, device_id_type=MESH
        )
        return carry

    def greet_rows(hop, carry):
        pl.semaphore_signal(
            barrier, inc=1, device_id={"rows": lax.rem(me_r + hop, ROWS)}, device_id_type=MESH
        )
        return carry

    lax.fori_loop(1, PTS, greet_pts, 0)
    lax.fori_loop(1, ROWS, greet_rows, 0)

    loads = [
        pltpu.make_async_copy(src, dst, load_sem.at[at])
        for at, (src, dst) in enumerate(
            [(w_hbm, w_ref), (z_hbm, z_ref), (t_hbm, t_ref), (core_hbm, core_ref)]
        )
    ]
    for load in loads:
        load.start()

    def wait_bytes(ref, sem):
        pltpu.make_async_copy(ref, ref, sem).wait()

    arrivals = {}
    sent = []

    def expect(sem, ref):
        arrivals[sem] = ref
        sent.append((sem, ref))

    def arrive(sem):
        wait_bytes(arrivals.pop(sem), recv_sem.at[sem])

    idx_ref[...] = jnp.zeros_like(idx_ref)
    for update in range(2):
        for group in range(ROWS):
            at = update * ROWS + group
            idx_ref[at : at + 1, :] = bi_ref[
                update : update + 1, group * GROUP : (group + 1) * GROUP
            ].astype(F32)
        own = pl.ds(pl.multiple_of(me_r * GROUP, GROUP), GROUP)
        idx_ref[16 + update : 17 + update, :] = bi_ref[update : update + 1, own].astype(F32)
        for half in range(2):
            at = 18 + update * 2 + half
            idx_ref[at : at + 1, :] = pv_ref[
                update : update + 1, half * GROUP : (half + 1) * GROUP
            ].astype(F32)
    idxt_ref[...] = jnp.transpose(idx_ref[...])

    below = iota((GROUP, GROUP), 1) < iota((GROUP, GROUP), 0)
    above = iota((GROUP, GROUP), 0) < iota((GROUP, GROUP), 1)
    ones_mat = jnp.ones((GROUP, 128), BF16)

    def owners(at):
        return owner_of(idxt_ref[:, at : at + 1]), owner_of(idx_ref[at : at + 1, :])

    def rank_col(at):
        col, row = owners(at)
        same = jnp.where((col == row) & below, 1.0, 0.0).astype(BF16)
        return dot(same, ones_mat)

    def rank_row(at):
        col, row = owners(at)
        same = jnp.where((col == row) & above, 1.0, 0.0).astype(BF16)
        return dot(jnp.ones((8, GROUP), BF16), same)

    for update in range(2):
        row = idx_ref[16 + update : 17 + update, :]
        rank = rank_row(16 + update)[0:1]
        slot = jnp.where(owner_of(row) == p_f, rank, -1.0)
        pick = jnp.where(iota((CAP, GROUP), 0) == slot, 1.0, 0.0).astype(BF16)
        col = idxt_ref[:, 16 + update : 17 + update] - p_f * LOCAL
        hot = jnp.where(iota((GROUP, LOCAL), 1) == col, 1.0, 0.0).astype(BF16)
        place = dot(pick, hot).astype(BF16)
        g_snd[update] = dot(place, x_ref[...]).astype(BF16)

    pl.semaphore_wait(barrier, PTS + ROWS - 2)

    def to_pts(src_of, dst, sem):
        def send(hop, carry):
            peer = lax.rem(me_p + hop, PTS)
            pltpu.make_async_remote_copy(
                src_ref=src_of(peer), dst_ref=dst.at[me_p],
                send_sem=send_sem.at[sem], recv_sem=recv_sem.at[sem],
                device_id={"pts": peer}, device_id_type=MESH,
            ).start()
            return carry

        lax.fori_loop(1, PTS, send, 0)
        expect(sem, dst.at[pl.ds(0, PTS - 1)])

    def to_rows(buf, sem):
        def send(hop, carry):
            peer = lax.rem(me_r + hop, ROWS)
            pltpu.make_async_remote_copy(
                src_ref=buf.at[me_r], dst_ref=buf.at[me_r],
                send_sem=send_sem.at[sem], recv_sem=recv_sem.at[sem],
                device_id={"rows": peer}, device_id_type=MESH,
            ).start()
            return carry

        lax.fori_loop(1, ROWS, send, 0)
        expect(sem, buf.at[pl.ds(0, ROWS - 1)])

    G, RS0, RS1, AX, DS, FX, FC = 0, 2, 3, 4, 6, 8, 10
    for update in range(2):
        to_pts(lambda peer: g_snd.at[update], g_rcv.at[update], G + update)
        g_rcv[update, me_p] = g_snd[update]

    loads[0].wait()
    loads[1].wait()
    w_now = w_ref[...]
    z_now = z_ref[...]
    mixed = alpha_mix * z_now + (1.0 - alpha_mix) * w_now
    base = alpha_mix * (beta_keep * z_now + (1.0 - beta_keep) * mixed) + (1.0 - alpha_mix) * mixed
    mixb_ref[...] = mixed.astype(BF16)
    baseb_ref[...] = base.astype(BF16)
    loads[2].wait()
    targets = t_ref[...].astype(F32)
    for update, value in enumerate((mixed, base)):
        wanted = ridge_term * value - targets
        high = wanted.astype(BF16)
        low = (wanted - high.astype(F32)).astype(BF16)
        col = idxt_ref[:, 16 + update : 17 + update] - p_f * LOCAL
        hot = jnp.where(iota((GROUP, LOCAL), 1) == col, 1.0, 0.0).astype(BF16)
        off_ref[update] = dot(hot, high) + dot(hot, low)

    x_sq = row_norms(x_ref[...])[0:1]

    def select_group(at, group_f, update):
        col = owner_of(idxt_ref[:, at : at + 1])
        quad = jnp.floor(col * 0.25)
        chunk = mod4(col - 4.0 * quad + group_f)
        slot = rank_col(at) + (quad * 128.0 + chunk * SLOTS)
        for block in range(ROWS):
            hit = iota((GROUP, 128), 1) + 128.0 * block == slot
            sel_ref[at, :, block * 128 : (block + 1) * 128] = jnp.where(hit, 1.0, 0.0).astype(BF16)

    for update in range(2):
        for group in range(ROWS):
            select_group(update * ROWS + group, float(group), update)

    my_quad = me_p // 4
    my_kind = p_f - 4.0 * my_quad.astype(F32)
    chunk_of = jnp.floor(iota((8, 128), 1) * (1.0 / SLOTS))
    places_ref[...] = jnp.zeros_like(places_ref)
    for update in range(2):
        for half in range(2):
            total = jnp.zeros((8, 128), F32)
            for part in range(4):
                group = half * 4 + part
                at = update * ROWS + group
                row = idx_ref[at : at + 1, :]
                inner = row - LOCAL * owner_of(row)
                upper = jnp.floor(inner * (1.0 / 32.0))
                lhs = jnp.concatenate(
                    [upper, inner - 32.0 * upper, jnp.ones_like(row), jnp.zeros((5, GROUP), F32)],
                    axis=0,
                ).astype(BF16)
                block = sel_ref[at, :, pl.ds(pl.multiple_of(my_quad * 128, 128), 128)]
                found = dot(lhs, block)
                total = jnp.where(chunk_of == mod4(my_kind + part), found, total)
            point = 32.0 * total[0:1] + total[1:2] - (1.0 - total[2:3])
            places_ref[update : update + 1, half * 128 : (half + 1) * 128] = point

    slots_iota = iota((GROUP, PTS * CAP), 1)
    for update in range(2):
        col = owner_of(idxt_ref[:, 16 + update : 17 + update])
        slot = rank_col(16 + update)[:, 0:1] + col * CAP
        own_sel_ref[update] = jnp.where(slots_iota == slot, 1.0, 0.0).astype(BF16)
        for half in range(2):
            at = 18 + update * 2 + half
            col = idxt_ref[:, at : at + 1]
            for group in range(ROWS):
                hit = iota((GROUP, GROUP), 1) + float(group * GROUP) == col
                pivot_sel_ref[update, half, :, group * GROUP : (group + 1) * GROUP] = jnp.where(
                    hit, 1.0, 0.0
                ).astype(BF16)

    def own_features(update):
        arrive(G + update)
        rows = dot(own_sel_ref[update], g_rcv[update].reshape(PTS * CAP, 128)).astype(BF16)
        feats_ref[update, core, chip] = rows
        for hop in range(1, 4):
            pltpu.make_async_remote_copy(
                src_ref=feats_ref.at[update, core, chip],
                dst_ref=feats_ref.at[update, core, chip],
                send_sem=send_sem.at[FX + update], recv_sem=recv_sem.at[FX + update],
                device_id={"rows": lax.rem(me_r + 2 * hop, ROWS)}, device_id_type=MESH,
            ).start()
        expect(FX + update, feats_ref.at[update, core, pl.ds(0, 3)])
        return rows

    def share_with_core(update):
        arrive(FX + update)
        pltpu.make_async_remote_copy(
            src_ref=feats_ref.at[update, core], dst_ref=feats_ref.at[update, core],
            send_sem=send_sem.at[FC + update], recv_sem=recv_sem.at[FC + update],
            device_id={"rows": chip * 2 + 1 - core}, device_id_type=MESH,
        ).start()
        expect(FC + update, feats_ref.at[update, core])

    def group_rows(update, group):
        return feats_ref[update, lax.rem(group, 2), group // 2]

    def partial_rows(rows, coefs, offset):
        tile = kernel_tile(rows, x_ref[...], x_sq)
        return dot(tile, coefs) + offset

    def put_pieces(dst, value):
        flipped = jnp.transpose(value)
        for piece in range(PTS):
            dst[piece] = stack(flipped[piece * 8 : piece * 8 + 8]).astype(BF16)

    rows0 = own_features(0)
    put_pieces(rs0_snd, partial_rows(rows0, mixb_ref[...], off_ref[0]))
    to_pts(lambda peer: rs0_snd.at[peer], rs0_rcv, RS0)
    rs0_rcv[me_p] = rs0_snd[me_p]

    rows1 = own_features(1)
    put_pieces(rs1_snd, partial_rows(rows1, baseb_ref[...], off_ref[1]))
    to_pts(lambda peer: rs1_snd.at[peer], rs1_rcv, RS1)
    rs1_rcv[me_p] = rs1_snd[me_p]

    def make_factor(update):
        arrive(FC + update)
        pivots = []
        for half in range(2):
            total = jnp.zeros((GROUP, 128), F32)
            for group in range(ROWS):
                hot = pivot_sel_ref[update, half, :, group * GROUP : (group + 1) * GROUP]
                total = total + dot(hot, feats_ref[update, group % 2, group // 2])
            pivots.append(total.astype(BF16))
        pivots = jnp.concatenate(pivots, axis=0)
        pivots_sq = row_norms(pivots)[0:1]

        def body(group, carry):
            at = pl.ds(pl.multiple_of(group * GROUP, GROUP), GROUP)
            factor_ref[update, at, :] = kernel_tile(group_rows(update, group), pivots, pivots_sq)
            return carry

        lax.fori_loop(0, ROWS, body, 0)

    def sum_pieces(rcv):
        total = rcv[0].astype(F32)
        for piece in range(1, PTS):
            total = total + rcv[piece].astype(F32)
        return total

    def share_rows(at, value):
        ax_ref[at, me_r] = value.astype(BF16)
        to_rows(ax_ref.at[at], AX + at)

    def whole_rows(at):
        arrive(AX + at)
        parts = []
        for group in range(ROWS):
            parts += unstack(ax_ref[at, group].astype(F32))
        return jnp.concatenate(parts, axis=1)

    rows1_sq = row_norms(rows1)[0:1]
    row1 = idx_ref[17:18, :]

    def cross_part(kind):
        for at in range(4):
            tile = kernel_tile(feats_ref[0, kind, at], rows1, rows1_sq)
            col = jnp.where(
                kind == 0, idxt_ref[:, 2 * at : 2 * at + 1], idxt_ref[:, 2 * at + 1 : 2 * at + 2]
            )
            same = jnp.where(col == row1, ridge_term, 0.0)
            rows = pl.ds(pl.multiple_of((2 * at + kind) * GROUP, GROUP), GROUP)
            cross_ref[rows, :] = (tile.astype(F32) + same).astype(BF16)

    share_with_core(0)
    cross_part(core)
    arrive(RS0)
    share_rows(0, sum_pieces(rs0_rcv))
    make_factor(0)
    share_with_core(1)
    cross_part(1 - core)
    loads[3].wait()

    def step_of(update, resid):
        proj = dot(resid.astype(BF16), factor_ref[update])
        lifted = dot(proj.astype(BF16), core_ref[update], NT).astype(BF16)
        return (resid - dot(lifted, factor_ref[update], NT)).astype(BF16)

    def send_steps(update, step):
        chunk_at = jnp.floor(iota((8, 128), 1) * (1.0 / SLOTS))
        for pair in range(4):
            cut = slice(pair * 256, pair * 256 + 256)
            found = [
                dot(
                    step[:, group * GROUP : (group + 1) * GROUP],
                    sel_ref[update * ROWS + group, :, cut],
                )
                for group in range(ROWS)
            ]
            for at in range(8):
                owner = pair * 8 + at
                halves = []
                for half in range(2):
                    total = jnp.zeros((8, 128), F32)
                    for part in range(4):
                        lanes = slice(at // 4 * 128, at // 4 * 128 + 128)
                        piece = found[half * 4 + part][:, lanes]
                        total = jnp.where(chunk_at == float((owner + part) % 4), piece, total)
                    halves.append(total)
                d_snd[update, owner] = jnp.concatenate(halves, axis=0).astype(BF16)
        to_pts(lambda peer: d_snd.at[update, peer], d_rcv.at[update], DS + update)
        d_rcv[update, me_p] = d_snd[update, me_p]

    def received(update):
        arrive(DS + update)
        halves = []
        for half in range(2):
            cut = slice(half * 8, half * 8 + 8)
            halves.append(
                jnp.concatenate(
                    [d_rcv[update, piece].astype(F32)[cut] for piece in range(PTS)], axis=0
                )
            )
        return jnp.concatenate(halves, axis=1).astype(BF16)

    step0 = step_of(0, whole_rows(0))
    drop = alpha_mix * step_size * momentum_gain + (1.0 - alpha_mix) * step_size
    change = dot(step0, cross_ref[...]) * drop
    arrive(RS1)
    share_rows(1, sum_pieces(rs1_rcv) - stack(change))
    send_steps(0, step0)
    make_factor(1)
    step1 = step_of(1, whole_rows(1))
    send_steps(1, step1)

    steps0 = received(0)
    for part in range(4):
        cut = slice(part * 256, part * 256 + 256)
        current, momentum_now = apply_update(
            w_ref[cut, :], z_ref[cut, :], steps0, places_ref[0:1, :], part * 256.0
        )
        w_ref[cut, :] = current
        z_ref[cut, :] = momentum_now
    stores = [
        pltpu.make_async_copy(src, dst, load_sem.at[at])
        for at, (src, dst) in enumerate([(w_ref, w_mid), (z_ref, z_mid)])
    ]
    for store in stores:
        store.start()
    steps_ref[...] = received(1)

    for store in stores:
        store.wait()
    for sem, ref in sent:
        wait_bytes(ref, send_sem.at[sem])


def apply_kernel(
    w_ref, z_ref, steps_hbm, places_hbm, w_out, z_out,
    w_now, z_now, steps_ref, places_ref, small_sem, load_sem, store_sem,
):
    tile = w_now.shape[0] // STORES
    loads = []
    stores = []
    small = [
        pltpu.make_async_copy(steps_hbm, steps_ref, small_sem.at[0]),
        pltpu.make_async_copy(places_hbm, places_ref, small_sem.at[1]),
    ]
    for load in small:
        load.start()
    for part in range(STORES):
        cut = pl.ds(part * tile, tile)
        for at, (src, dst) in enumerate([(w_ref, w_now), (z_ref, z_now)]):
            loads.append(pltpu.make_async_copy(src.at[cut], dst.at[cut], load_sem.at[at, part]))
            loads[-1].start()
    for load in small:
        load.wait()
    for part in range(STORES):
        cut = pl.ds(part * tile, tile)
        loads[2 * part].wait()
        loads[2 * part + 1].wait()
        current, momentum_now = apply_update(
            w_now[cut, :], z_now[cut, :], steps_ref[...], places_ref[1:2, :], float(part * tile)
        )
        w_now[cut, :] = current
        z_now[cut, :] = momentum_now
        for at, (src, dst) in enumerate([(w_now, w_out), (z_now, z_out)]):
            stores.append(pltpu.make_async_copy(src.at[cut], dst.at[cut], store_sem.at[at, part]))
            stores[-1].start()
    for store in stores:
        store.wait()


def shards(features, targets, coefficients, momentum, block_index, pivot_index, nystrom_core):
    vmem = pl.BlockSpec(memory_space=pltpu.VMEM)
    anywhere = pl.BlockSpec(memory_space=pl.ANY)
    hbm = pl.BlockSpec(memory_space=pltpu.HBM)
    w_mid, z_mid, steps, places = pl.pallas_call(
        block_kernel,
        out_shape=(
            jax.ShapeDtypeStruct(coefficients.shape, F32),
            jax.ShapeDtypeStruct(momentum.shape, F32),
            jax.ShapeDtypeStruct((256, GROUP), BF16),
            jax.ShapeDtypeStruct((8, GROUP), F32),
        ),
        in_specs=[vmem, vmem, vmem, hbm, hbm, hbm, hbm],
        out_specs=(anywhere, anywhere, vmem, vmem),
        scratch_shapes=[
            pltpu.VMEM((128, GROUP), F32),
            pltpu.VMEM((GROUP, 128), F32),
            pltpu.VMEM((LOCAL, 256), F32),
            pltpu.VMEM((LOCAL, 256), F32),
            pltpu.VMEM((LOCAL, 256), BF16),
            pltpu.VMEM((2, 512, 512), BF16),
            pltpu.SemaphoreType.DMA((4,)),
            pltpu.VMEM((16, GROUP, PTS * SLOTS), BF16),
            pltpu.VMEM((2, GROUP, PTS * CAP), BF16),
            pltpu.VMEM((2, 2, GROUP, ROWS * GROUP), BF16),
            pltpu.VMEM((2, CAP, 128), BF16),
            pltpu.VMEM((2, PTS, CAP, 128), BF16),
            pltpu.VMEM((2, 2, 4, GROUP, 128), BF16),
            pltpu.VMEM((2, ROWS * GROUP, 512), BF16),
            pltpu.VMEM((ROWS * GROUP, GROUP), BF16),
            pltpu.VMEM((LOCAL, 256), BF16),
            pltpu.VMEM((LOCAL, 256), BF16),
            pltpu.VMEM((2, GROUP, 256), F32),
            pltpu.VMEM((PTS, 16, 128), BF16),
            pltpu.VMEM((PTS, 16, 128), BF16),
            pltpu.VMEM((PTS, 16, 128), BF16),
            pltpu.VMEM((PTS, 16, 128), BF16),
            pltpu.VMEM((2, ROWS, 16, 128), BF16),
            pltpu.VMEM((2, PTS, 16, 128), BF16),
            pltpu.VMEM((2, PTS, 16, 128), BF16),
            pltpu.SemaphoreType.DMA((12,)),
            pltpu.SemaphoreType.DMA((12,)),
        ],
        compiler_params=pltpu.CompilerParams(
            collective_id=0, has_side_effects=True, vmem_limit_bytes=VMEM_BYTES
        ),
        name="block_steps",
    )(block_index, pivot_index, features, coefficients, momentum, targets, nystrom_core)

    return pl.pallas_call(
        apply_kernel,
        out_shape=(
            jax.ShapeDtypeStruct(coefficients.shape, F32),
            jax.ShapeDtypeStruct(momentum.shape, F32),
        ),
        in_specs=[hbm, hbm, hbm, hbm],
        out_specs=(hbm, hbm),
        scratch_shapes=[
            pltpu.VMEM((LOCAL, 256), F32),
            pltpu.VMEM((LOCAL, 256), F32),
            pltpu.VMEM((256, GROUP), BF16),
            pltpu.VMEM((8, GROUP), F32),
            pltpu.SemaphoreType.DMA((2,)),
            pltpu.SemaphoreType.DMA((2, STORES)),
            pltpu.SemaphoreType.DMA((2, STORES)),
        ],
        compiler_params=pltpu.CompilerParams(vmem_limit_bytes=VMEM_BYTES),
        name="apply_steps",
    )(w_mid, z_mid, steps, places)


def solution(mesh):
    in_specs = (P("pts", None), P("pts", None), P("pts", None), P("pts", None), P(), P(), P())
    out_specs = (P("pts", None), P("pts", None))
    return jax.shard_map(shards, mesh=mesh, in_specs=in_specs, out_specs=out_specs, check_vma=False)
```

```python
import functools

import jax
import jax.numpy as jnp
from jax import lax
from jax.experimental import pallas as pl
from jax.experimental.pallas import tpu as pltpu
from jax.sharding import PartitionSpec as P

alpha_mix = 0.6
beta_keep = 0.9
step_size = 0.2
momentum_gain = 1.5
ridge_term = 1.0

F32 = jnp.float32
BF16 = jnp.bfloat16
NN = (((1,), (0,)), ((), ()))
NT = (((1,), (1,)), ((), ()))
MESH = pl.DeviceIdType.MESH

PTS = 32
ROWS = 8
LOCAL = 1024
GROUP = 256
CAP = 24
VMEM_BYTES = 64_500_000
STORES = 2
SLOTS = 32


def dot(left, right, dims=NN):
    return lax.dot_general(left, right, dims, preferred_element_type=F32)


def row_norms(rows):
    squares = jnp.square(rows.astype(F32))
    high = squares.astype(BF16)
    low = (squares - high.astype(F32)).astype(BF16)
    ones = jnp.ones((8, rows.shape[1]), BF16)
    return dot(ones, high, NT) + dot(ones, low, NT)


def kernel_tile(left, right, right_sq):
    scale = -3.5 / left.shape[1]
    left_sq = jnp.sum(jnp.square(left.astype(F32)), axis=1, keepdims=True)
    squared = left_sq + right_sq - 2.0 * dot(left, right, NT)
    return jnp.exp(squared * scale).astype(BF16)


def iota(shape, axis):
    return lax.broadcasted_iota(jnp.int32, shape, axis).astype(F32)


def owner_of(index):
    return jnp.floor(index * (1.0 / LOCAL))


def mod4(value):
    return value - 4.0 * jnp.floor(value * 0.25)


def stack(value):
    return jnp.concatenate([value[:, :128], value[:, 128:]], axis=0)


def unstack(value):
    return [value[:8], value[8:]]


def apply_update(current, momentum_now, steps, place, first):
    hot = jnp.where(iota((current.shape[0], GROUP), 0) + first == place, 1.0, 0.0).astype(BF16)
    delta = dot(hot, steps, NT)
    mixed = alpha_mix * momentum_now + (1.0 - alpha_mix) * current
    current = mixed - step_size * delta
    momentum_now = (
        beta_keep * momentum_now + (1.0 - beta_keep) * mixed
    ) - step_size * momentum_gain * delta
    return current, momentum_now


def block_kernel(
    bi_ref, pv_ref, x_ref, w_hbm, z_hbm, t_hbm, core_hbm,
    w_mid, z_mid, steps_ref, places_ref,
    idx_ref, idxt_ref, w_ref, z_ref, t_ref, core_ref, load_sem,
    sel_ref, own_sel_ref, pivot_sel_ref, g_snd, g_rcv, feats_ref, factor_ref, cross_ref, mixb_ref, baseb_ref,
    off_ref, rs0_snd, rs0_rcv, rs1_snd, rs1_rcv, ax_ref, d_snd, d_rcv,
    send_sem, recv_sem,
):
    me_r = lax.axis_index("rows")
    me_p = lax.axis_index("pts")
    core = lax.rem(me_r, 2)
    chip = me_r // 2
    p_f = me_p.astype(F32)
    r_f = me_r.astype(F32)

    barrier = pltpu.get_barrier_semaphore()

    def greet_pts(hop, carry):
        pl.semaphore_signal(
            barrier, inc=1, device_id={"pts": lax.rem(me_p + hop, PTS)}, device_id_type=MESH
        )
        return carry

    def greet_rows(hop, carry):
        pl.semaphore_signal(
            barrier, inc=1, device_id={"rows": lax.rem(me_r + hop, ROWS)}, device_id_type=MESH
        )
        return carry

    lax.fori_loop(1, PTS, greet_pts, 0)
    lax.fori_loop(1, ROWS, greet_rows, 0)

    loads = [
        pltpu.make_async_copy(src, dst, load_sem.at[at])
        for at, (src, dst) in enumerate(
            [(w_hbm, w_ref), (z_hbm, z_ref), (t_hbm, t_ref), (core_hbm, core_ref)]
        )
    ]
    for load in loads:
        load.start()

    def wait_bytes(ref, sem):
        pltpu.make_async_copy(ref, ref, sem).wait()

    arrivals = {}
    sent = []

    def expect(sem, ref):
        arrivals[sem] = ref
        sent.append((sem, ref))

    def arrive(sem):
        wait_bytes(arrivals.pop(sem), recv_sem.at[sem])

    idx_ref[...] = jnp.zeros_like(idx_ref)
    for update in range(2):
        for group in range(ROWS):
            at = update * ROWS + group
            idx_ref[at : at + 1, :] = bi_ref[
                update : update + 1, group * GROUP : (group + 1) * GROUP
            ].astype(F32)
        own = pl.ds(pl.multiple_of(me_r * GROUP, GROUP), GROUP)
        idx_ref[16 + update : 17 + update, :] = bi_ref[update : update + 1, own].astype(F32)
        for half in range(2):
            at = 18 + update * 2 + half
            idx_ref[at : at + 1, :] = pv_ref[
                update : update + 1, half * GROUP : (half + 1) * GROUP
            ].astype(F32)
    idxt_ref[...] = jnp.transpose(idx_ref[...])

    below = iota((GROUP, GROUP), 1) < iota((GROUP, GROUP), 0)
    above = iota((GROUP, GROUP), 0) < iota((GROUP, GROUP), 1)
    ones_mat = jnp.ones((GROUP, 128), BF16)

    def owners(at):
        return owner_of(idxt_ref[:, at : at + 1]), owner_of(idx_ref[at : at + 1, :])

    def rank_col(at):
        col, row = owners(at)
        same = jnp.where((col == row) & below, 1.0, 0.0).astype(BF16)
        return dot(same, ones_mat)

    def rank_row(at):
        col, row = owners(at)
        same = jnp.where((col == row) & above, 1.0, 0.0).astype(BF16)
        return dot(jnp.ones((8, GROUP), BF16), same)

    for update in range(2):
        row = idx_ref[16 + update : 17 + update, :]
        rank = rank_row(16 + update)[0:1]
        slot = jnp.where(owner_of(row) == p_f, rank, -1.0)
        pick = jnp.where(iota((CAP, GROUP), 0) == slot, 1.0, 0.0).astype(BF16)
        col = idxt_ref[:, 16 + update : 17 + update] - p_f * LOCAL
        hot = jnp.where(iota((GROUP, LOCAL), 1) == col, 1.0, 0.0).astype(BF16)
        place = dot(pick, hot).astype(BF16)
        g_snd[update] = dot(place, x_ref[...]).astype(BF16)

    pl.semaphore_wait(barrier, PTS + ROWS - 2)

    deep = PTS // 4
    peer_y = [lax.rem(me_p // deep + step, 4) * deep for step in range(4)]
    peer_z = [lax.rem(me_p + step, deep) for step in range(deep)]
    farthest_first = sorted(
        ((step, hop) for step in range(4) for hop in range(deep) if step or hop),
        key=lambda at: -min(at[0], 4 - at[0]) - min(at[1], deep - at[1]),
    )

    def to_pts(src_of, dst, sem):
        for step, hop in farthest_first:
            peer = peer_y[step] + peer_z[hop]
            pltpu.make_async_remote_copy(
                src_ref=src_of(peer), dst_ref=dst.at[me_p],
                send_sem=send_sem.at[sem], recv_sem=recv_sem.at[sem],
                device_id={"pts": peer}, device_id_type=MESH,
            ).start()
        expect(sem, dst.at[pl.ds(0, PTS - 1)])

    def to_rows(buf, sem):
        def send(hop, carry):
            peer = lax.rem(me_r + hop, ROWS)
            pltpu.make_async_remote_copy(
                src_ref=buf.at[me_r], dst_ref=buf.at[me_r],
                send_sem=send_sem.at[sem], recv_sem=recv_sem.at[sem],
                device_id={"rows": peer}, device_id_type=MESH,
            ).start()
            return carry

        lax.fori_loop(1, ROWS, send, 0)
        expect(sem, buf.at[pl.ds(0, ROWS - 1)])

    G, RS0, RS1, AX, DS, FX, FC = 0, 2, 3, 4, 6, 8, 10
    for update in range(2):
        to_pts(lambda peer: g_snd.at[update], g_rcv.at[update], G + update)
        g_rcv[update, me_p] = g_snd[update]

    loads[0].wait()
    loads[1].wait()
    w_now = w_ref[...]
    z_now = z_ref[...]
    mixed = alpha_mix * z_now + (1.0 - alpha_mix) * w_now
    base = alpha_mix * (beta_keep * z_now + (1.0 - beta_keep) * mixed) + (1.0 - alpha_mix) * mixed
    mixb_ref[...] = mixed.astype(BF16)
    baseb_ref[...] = base.astype(BF16)
    loads[2].wait()
    targets = t_ref[...].astype(F32)
    for update, value in enumerate((mixed, base)):
        wanted = ridge_term * value - targets
        high = wanted.astype(BF16)
        low = (wanted - high.astype(F32)).astype(BF16)
        col = idxt_ref[:, 16 + update : 17 + update] - p_f * LOCAL
        hot = jnp.where(iota((GROUP, LOCAL), 1) == col, 1.0, 0.0).astype(BF16)
        off_ref[update] = dot(hot, high) + dot(hot, low)

    x_sq = row_norms(x_ref[...])[0:1]

    def select_group(at, group_f, update):
        col = owner_of(idxt_ref[:, at : at + 1])
        quad = jnp.floor(col * 0.25)
        chunk = mod4(col - 4.0 * quad + group_f)
        slot = rank_col(at) + (quad * 128.0 + chunk * SLOTS)
        for block in range(ROWS):
            hit = iota((GROUP, 128), 1) + 128.0 * block == slot
            sel_ref[at, :, block * 128 : (block + 1) * 128] = jnp.where(hit, 1.0, 0.0).astype(BF16)

    for update in range(2):
        for group in range(ROWS):
            select_group(update * ROWS + group, float(group), update)

    my_quad = me_p // 4
    my_kind = p_f - 4.0 * my_quad.astype(F32)
    chunk_of = jnp.floor(iota((8, 128), 1) * (1.0 / SLOTS))
    places_ref[...] = jnp.zeros_like(places_ref)
    for update in range(2):
        for half in range(2):
            total = jnp.zeros((8, 128), F32)
            for part in range(4):
                group = half * 4 + part
                at = update * ROWS + group
                row = idx_ref[at : at + 1, :]
                inner = row - LOCAL * owner_of(row)
                upper = jnp.floor(inner * (1.0 / 32.0))
                lhs = jnp.concatenate(
                    [upper, inner - 32.0 * upper, jnp.ones_like(row), jnp.zeros((5, GROUP), F32)],
                    axis=0,
                ).astype(BF16)
                block = sel_ref[at, :, pl.ds(pl.multiple_of(my_quad * 128, 128), 128)]
                found = dot(lhs, block)
                total = jnp.where(chunk_of == mod4(my_kind + part), found, total)
            point = 32.0 * total[0:1] + total[1:2] - (1.0 - total[2:3])
            places_ref[update : update + 1, half * 128 : (half + 1) * 128] = point

    slots_iota = iota((GROUP, PTS * CAP), 1)
    for update in range(2):
        col = owner_of(idxt_ref[:, 16 + update : 17 + update])
        slot = rank_col(16 + update)[:, 0:1] + col * CAP
        own_sel_ref[update] = jnp.where(slots_iota == slot, 1.0, 0.0).astype(BF16)
        for half in range(2):
            at = 18 + update * 2 + half
            col = idxt_ref[:, at : at + 1]
            for group in range(ROWS):
                hit = iota((GROUP, GROUP), 1) + float(group * GROUP) == col
                pivot_sel_ref[update, half, :, group * GROUP : (group + 1) * GROUP] = jnp.where(
                    hit, 1.0, 0.0
                ).astype(BF16)

    def own_features(update):
        arrive(G + update)
        rows = dot(own_sel_ref[update], g_rcv[update].reshape(PTS * CAP, 128)).astype(BF16)
        feats_ref[update, core, chip] = rows
        for hop in range(1, 4):
            pltpu.make_async_remote_copy(
                src_ref=feats_ref.at[update, core, chip],
                dst_ref=feats_ref.at[update, core, chip],
                send_sem=send_sem.at[FX + update], recv_sem=recv_sem.at[FX + update],
                device_id={"rows": lax.rem(me_r + 2 * hop, ROWS)}, device_id_type=MESH,
            ).start()
        expect(FX + update, feats_ref.at[update, core, pl.ds(0, 3)])
        return rows

    def share_with_core(update):
        arrive(FX + update)
        pltpu.make_async_remote_copy(
            src_ref=feats_ref.at[update, core], dst_ref=feats_ref.at[update, core],
            send_sem=send_sem.at[FC + update], recv_sem=recv_sem.at[FC + update],
            device_id={"rows": chip * 2 + 1 - core}, device_id_type=MESH,
        ).start()
        expect(FC + update, feats_ref.at[update, core])

    def group_rows(update, group):
        return feats_ref[update, lax.rem(group, 2), group // 2]

    def partial_rows(rows, coefs, offset):
        tile = kernel_tile(rows, x_ref[...], x_sq)
        return dot(tile, coefs) + offset

    def put_pieces(dst, value):
        flipped = jnp.transpose(value)
        for piece in range(PTS):
            dst[piece] = stack(flipped[piece * 8 : piece * 8 + 8]).astype(BF16)

    rows0 = own_features(0)
    put_pieces(rs0_snd, partial_rows(rows0, mixb_ref[...], off_ref[0]))
    to_pts(lambda peer: rs0_snd.at[peer], rs0_rcv, RS0)
    rs0_rcv[me_p] = rs0_snd[me_p]

    rows1 = own_features(1)
    put_pieces(rs1_snd, partial_rows(rows1, baseb_ref[...], off_ref[1]))
    to_pts(lambda peer: rs1_snd.at[peer], rs1_rcv, RS1)
    rs1_rcv[me_p] = rs1_snd[me_p]

    def make_factor(update):
        arrive(FC + update)
        pivots = []
        for half in range(2):
            total = jnp.zeros((GROUP, 128), F32)
            for group in range(ROWS):
                hot = pivot_sel_ref[update, half, :, group * GROUP : (group + 1) * GROUP]
                total = total + dot(hot, feats_ref[update, group % 2, group // 2])
            pivots.append(total.astype(BF16))
        pivots = jnp.concatenate(pivots, axis=0)
        pivots_sq = row_norms(pivots)[0:1]

        def body(group, carry):
            at = pl.ds(pl.multiple_of(group * GROUP, GROUP), GROUP)
            factor_ref[update, at, :] = kernel_tile(group_rows(update, group), pivots, pivots_sq)
            return carry

        lax.fori_loop(0, ROWS, body, 0)

    def sum_pieces(rcv):
        total = rcv[0].astype(F32)
        for piece in range(1, PTS):
            total = total + rcv[piece].astype(F32)
        return total

    def share_rows(at, value):
        ax_ref[at, me_r] = value.astype(BF16)
        to_rows(ax_ref.at[at], AX + at)

    def whole_rows(at):
        arrive(AX + at)
        parts = []
        for group in range(ROWS):
            parts += unstack(ax_ref[at, group].astype(F32))
        return jnp.concatenate(parts, axis=1)

    rows1_sq = row_norms(rows1)[0:1]
    row1 = idx_ref[17:18, :]

    def cross_part(kind):
        for at in range(4):
            tile = kernel_tile(feats_ref[0, kind, at], rows1, rows1_sq)
            col = jnp.where(
                kind == 0, idxt_ref[:, 2 * at : 2 * at + 1], idxt_ref[:, 2 * at + 1 : 2 * at + 2]
            )
            same = jnp.where(col == row1, ridge_term, 0.0)
            rows = pl.ds(pl.multiple_of((2 * at + kind) * GROUP, GROUP), GROUP)
            cross_ref[rows, :] = (tile.astype(F32) + same).astype(BF16)

    share_with_core(0)
    cross_part(core)
    arrive(RS0)
    share_rows(0, sum_pieces(rs0_rcv))
    make_factor(0)
    share_with_core(1)
    cross_part(1 - core)
    loads[3].wait()

    def step_of(update, resid):
        proj = dot(resid.astype(BF16), factor_ref[update])
        lifted = dot(proj.astype(BF16), core_ref[update], NT).astype(BF16)
        return (resid - dot(lifted, factor_ref[update], NT)).astype(BF16)

    def send_steps(update, step):
        chunk_at = jnp.floor(iota((8, 128), 1) * (1.0 / SLOTS))
        for pair in range(4):
            cut = slice(pair * 256, pair * 256 + 256)
            found = [
                dot(
                    step[:, group * GROUP : (group + 1) * GROUP],
                    sel_ref[update * ROWS + group, :, cut],
                )
                for group in range(ROWS)
            ]
            for at in range(8):
                owner = pair * 8 + at
                halves = []
                for half in range(2):
                    total = jnp.zeros((8, 128), F32)
                    for part in range(4):
                        lanes = slice(at // 4 * 128, at // 4 * 128 + 128)
                        piece = found[half * 4 + part][:, lanes]
                        total = jnp.where(chunk_at == float((owner + part) % 4), piece, total)
                    halves.append(total)
                d_snd[update, owner] = jnp.concatenate(halves, axis=0).astype(BF16)
        to_pts(lambda peer: d_snd.at[update].at[peer], d_rcv.at[update], DS + update)
        d_rcv[update, me_p] = d_snd[update, me_p]

    def received(update):
        arrive(DS + update)
        halves = []
        for half in range(2):
            cut = slice(half * 8, half * 8 + 8)
            halves.append(
                jnp.concatenate(
                    [d_rcv[update, piece].astype(F32)[cut] for piece in range(PTS)], axis=0
                )
            )
        return jnp.concatenate(halves, axis=1).astype(BF16)

    step0 = step_of(0, whole_rows(0))
    drop = alpha_mix * step_size * momentum_gain + (1.0 - alpha_mix) * step_size
    change = dot(step0, cross_ref[...]) * drop
    arrive(RS1)
    share_rows(1, sum_pieces(rs1_rcv) - stack(change))
    send_steps(0, step0)
    make_factor(1)
    step1 = step_of(1, whole_rows(1))
    send_steps(1, step1)

    steps0 = received(0)
    for part in range(4):
        cut = slice(part * 256, part * 256 + 256)
        current, momentum_now = apply_update(
            w_ref[cut, :], z_ref[cut, :], steps0, places_ref[0:1, :], part * 256.0
        )
        w_ref[cut, :] = current
        z_ref[cut, :] = momentum_now
    stores = [
        pltpu.make_async_copy(src, dst, load_sem.at[at])
        for at, (src, dst) in enumerate([(w_ref, w_mid), (z_ref, z_mid)])
    ]
    for store in stores:
        store.start()
    steps_ref[...] = received(1)

    for store in stores:
        store.wait()
    for sem, ref in sent:
        wait_bytes(ref, send_sem.at[sem])


def apply_kernel(
    w_ref, z_ref, steps_hbm, places_hbm, w_out, z_out,
    w_now, z_now, steps_ref, places_ref, small_sem, load_sem, store_sem,
):
    tile = w_now.shape[0] // STORES
    loads = []
    stores = []
    small = [
        pltpu.make_async_copy(steps_hbm, steps_ref, small_sem.at[0]),
        pltpu.make_async_copy(places_hbm, places_ref, small_sem.at[1]),
    ]
    for load in small:
        load.start()
    for part in range(STORES):
        cut = pl.ds(part * tile, tile)
        for at, (src, dst) in enumerate([(w_ref, w_now), (z_ref, z_now)]):
            loads.append(pltpu.make_async_copy(src.at[cut], dst.at[cut], load_sem.at[at, part]))
            loads[-1].start()
    for load in small:
        load.wait()
    for part in range(STORES):
        cut = pl.ds(part * tile, tile)
        loads[2 * part].wait()
        loads[2 * part + 1].wait()
        current, momentum_now = apply_update(
            w_now[cut, :], z_now[cut, :], steps_ref[...], places_ref[1:2, :], float(part * tile)
        )
        w_now[cut, :] = current
        z_now[cut, :] = momentum_now
        for at, (src, dst) in enumerate([(w_now, w_out), (z_now, z_out)]):
            stores.append(pltpu.make_async_copy(src.at[cut], dst.at[cut], store_sem.at[at, part]))
            stores[-1].start()
    for store in stores:
        store.wait()


def shards(features, targets, coefficients, momentum, block_index, pivot_index, nystrom_core):
    vmem = pl.BlockSpec(memory_space=pltpu.VMEM)
    anywhere = pl.BlockSpec(memory_space=pl.ANY)
    hbm = pl.BlockSpec(memory_space=pltpu.HBM)
    w_mid, z_mid, steps, places = pl.pallas_call(
        block_kernel,
        out_shape=(
            jax.ShapeDtypeStruct(coefficients.shape, F32),
            jax.ShapeDtypeStruct(momentum.shape, F32),
            jax.ShapeDtypeStruct((256, GROUP), BF16),
            jax.ShapeDtypeStruct((8, GROUP), F32),
        ),
        in_specs=[vmem, vmem, vmem, hbm, hbm, hbm, hbm],
        out_specs=(anywhere, anywhere, vmem, vmem),
        scratch_shapes=[
            pltpu.VMEM((128, GROUP), F32),
            pltpu.VMEM((GROUP, 128), F32),
            pltpu.VMEM((LOCAL, 256), F32),
            pltpu.VMEM((LOCAL, 256), F32),
            pltpu.VMEM((LOCAL, 256), BF16),
            pltpu.VMEM((2, 512, 512), BF16),
            pltpu.SemaphoreType.DMA((4,)),
            pltpu.VMEM((16, GROUP, PTS * SLOTS), BF16),
            pltpu.VMEM((2, GROUP, PTS * CAP), BF16),
            pltpu.VMEM((2, 2, GROUP, ROWS * GROUP), BF16),
            pltpu.VMEM((2, CAP, 128), BF16),
            pltpu.VMEM((2, PTS, CAP, 128), BF16),
            pltpu.VMEM((2, 2, 4, GROUP, 128), BF16),
            pltpu.VMEM((2, ROWS * GROUP, 512), BF16),
            pltpu.VMEM((ROWS * GROUP, GROUP), BF16),
            pltpu.VMEM((LOCAL, 256), BF16),
            pltpu.VMEM((LOCAL, 256), BF16),
            pltpu.VMEM((2, GROUP, 256), F32),
            pltpu.VMEM((PTS, 16, 128), BF16),
            pltpu.VMEM((PTS, 16, 128), BF16),
            pltpu.VMEM((PTS, 16, 128), BF16),
            pltpu.VMEM((PTS, 16, 128), BF16),
            pltpu.VMEM((2, ROWS, 16, 128), BF16),
            pltpu.VMEM((2, PTS, 16, 128), BF16),
            pltpu.VMEM((2, PTS, 16, 128), BF16),
            pltpu.SemaphoreType.DMA((12,)),
            pltpu.SemaphoreType.DMA((12,)),
        ],
        compiler_params=pltpu.CompilerParams(
            collective_id=0, has_side_effects=True, vmem_limit_bytes=VMEM_BYTES
        ),
        name="block_steps",
    )(block_index, pivot_index, features, coefficients, momentum, targets, nystrom_core)

    return pl.pallas_call(
        apply_kernel,
        out_shape=(
            jax.ShapeDtypeStruct(coefficients.shape, F32),
            jax.ShapeDtypeStruct(momentum.shape, F32),
        ),
        in_specs=[hbm, hbm, hbm, hbm],
        out_specs=(hbm, hbm),
        scratch_shapes=[
            pltpu.VMEM((LOCAL, 256), F32),
            pltpu.VMEM((LOCAL, 256), F32),
            pltpu.VMEM((256, GROUP), BF16),
            pltpu.VMEM((8, GROUP), F32),
            pltpu.SemaphoreType.DMA((2,)),
            pltpu.SemaphoreType.DMA((2, STORES)),
            pltpu.SemaphoreType.DMA((2, STORES)),
        ],
        compiler_params=pltpu.CompilerParams(vmem_limit_bytes=VMEM_BYTES),
        name="apply_steps",
    )(w_mid, z_mid, steps, places)


def solution(mesh):
    in_specs = (P("pts", None), P("pts", None), P("pts", None), P("pts", None), P(), P(), P())
    out_specs = (P("pts", None), P("pts", None))
    return jax.shard_map(shards, mesh=mesh, in_specs=in_specs, out_specs=out_specs, check_vma=False)
```

```python
import functools

import jax
import jax.numpy as jnp
from jax import lax
from jax.experimental import pallas as pl
from jax.experimental.pallas import tpu as pltpu
from jax.sharding import PartitionSpec as P

alpha_mix = 0.6
beta_keep = 0.9
step_size = 0.2
momentum_gain = 1.5
ridge_term = 1.0

F32 = jnp.float32
BF16 = jnp.bfloat16
NN = (((1,), (0,)), ((), ()))
NT = (((1,), (1,)), ((), ()))
MESH = pl.DeviceIdType.MESH

PTS = 32
ROWS = 8
LOCAL = 1024
GROUP = 256
CAP = 24
VMEM_BYTES = 64_500_000
STORES = 2
SLOTS = 32


def dot(left, right, dims=NN):
    return lax.dot_general(left, right, dims, preferred_element_type=F32)


def row_norms(rows):
    squares = jnp.square(rows.astype(F32))
    high = squares.astype(BF16)
    low = (squares - high.astype(F32)).astype(BF16)
    ones = jnp.ones((8, rows.shape[1]), BF16)
    return dot(ones, high, NT) + dot(ones, low, NT)


def kernel_tile(left, right, right_sq):
    scale = -3.5 / left.shape[1]
    left_sq = jnp.sum(jnp.square(left.astype(F32)), axis=1, keepdims=True)
    squared = left_sq + right_sq - 2.0 * dot(left, right, NT)
    return jnp.exp(squared * scale).astype(BF16)


def iota(shape, axis):
    return lax.broadcasted_iota(jnp.int32, shape, axis).astype(F32)


def owner_of(index):
    return jnp.floor(index * (1.0 / LOCAL))


def mod4(value):
    return value - 4.0 * jnp.floor(value * 0.25)


def stack(value):
    return jnp.concatenate([value[:, :128], value[:, 128:]], axis=0)


def unstack(value):
    return [value[:8], value[8:]]


def apply_update(current, momentum_now, steps, place, first):
    hot = jnp.where(iota((current.shape[0], GROUP), 0) + first == place, 1.0, 0.0).astype(BF16)
    delta = dot(hot, steps, NT)
    mixed = alpha_mix * momentum_now + (1.0 - alpha_mix) * current
    current = mixed - step_size * delta
    momentum_now = (
        beta_keep * momentum_now + (1.0 - beta_keep) * mixed
    ) - step_size * momentum_gain * delta
    return current, momentum_now


def block_kernel(
    bi_hbm, pv_hbm, x_hbm, w_hbm, z_hbm, t_hbm, core_hbm,
    w_mid, z_mid, steps_ref, places_ref,
    bi_ref, pv_ref, x_ref, idx_ref, idxt_ref, w_ref, z_ref, t_ref, core_ref, load_sem,
    sel_ref, own_sel_ref, pivot_sel_ref, g_snd, g_rcv, feats_ref, factor_ref, cross_ref, mixb_ref, baseb_ref,
    off_ref, rs0_snd, rs0_rcv, rs1_snd, rs1_rcv, ax_ref, d_snd, d_rcv,
    send_sem, recv_sem,
):
    me_r = lax.axis_index("rows")
    me_p = lax.axis_index("pts")
    core = lax.rem(me_r, 2)
    chip = me_r // 2
    p_f = me_p.astype(F32)
    r_f = me_r.astype(F32)

    barrier = pltpu.get_barrier_semaphore()

    first_loads = [
        pltpu.make_async_copy(src, dst, load_sem.at[4 + at])
        for at, (src, dst) in enumerate([(bi_hbm, bi_ref), (pv_hbm, pv_ref), (x_hbm, x_ref)])
    ]
    for load in first_loads:
        load.start()

    deep = PTS // 4
    peer_y = [lax.rem(me_p // deep + step, 4) * deep for step in range(4)]
    peer_z = [lax.rem(me_p + step, deep) for step in range(deep)]
    farthest_first = sorted(
        ((step, hop) for step in range(4) for hop in range(deep) if step or hop),
        key=lambda at: -min(at[0], 4 - at[0]) - min(at[1], deep - at[1]),
    )

    def greet_rows(hop, carry):
        pl.semaphore_signal(
            barrier, inc=1, device_id={"rows": lax.rem(me_r + hop, ROWS)}, device_id_type=MESH
        )
        return carry

    for step, hop in farthest_first:
        pl.semaphore_signal(
            barrier, inc=1, device_id={"pts": peer_y[step] + peer_z[hop]}, device_id_type=MESH
        )
    lax.fori_loop(1, ROWS, greet_rows, 0)

    loads = [
        pltpu.make_async_copy(src, dst, load_sem.at[at])
        for at, (src, dst) in enumerate(
            [(w_hbm, w_ref), (z_hbm, z_ref), (t_hbm, t_ref), (core_hbm, core_ref)]
        )
    ]
    for load in loads:
        load.start()

    def wait_bytes(ref, sem):
        pltpu.make_async_copy(ref, ref, sem).wait()

    arrivals = {}
    sent = []

    def expect(sem, ref):
        arrivals[sem] = ref
        sent.append((sem, ref))

    def arrive(sem):
        wait_bytes(arrivals.pop(sem), recv_sem.at[sem])

    idx_ref[...] = jnp.zeros_like(idx_ref)
    for load in first_loads:
        load.wait()
    for update in range(2):
        for group in range(ROWS):
            at = update * ROWS + group
            idx_ref[at : at + 1, :] = bi_ref[
                update : update + 1, group * GROUP : (group + 1) * GROUP
            ].astype(F32)
        own = pl.ds(pl.multiple_of(me_r * GROUP, GROUP), GROUP)
        idx_ref[16 + update : 17 + update, :] = bi_ref[update : update + 1, own].astype(F32)
        for half in range(2):
            at = 18 + update * 2 + half
            idx_ref[at : at + 1, :] = pv_ref[
                update : update + 1, half * GROUP : (half + 1) * GROUP
            ].astype(F32)
    idxt_ref[...] = jnp.transpose(idx_ref[...])

    below = iota((GROUP, GROUP), 1) < iota((GROUP, GROUP), 0)
    above = iota((GROUP, GROUP), 0) < iota((GROUP, GROUP), 1)
    ones_mat = jnp.ones((GROUP, 128), BF16)

    def owners(at):
        return owner_of(idxt_ref[:, at : at + 1]), owner_of(idx_ref[at : at + 1, :])

    def rank_col(at):
        col, row = owners(at)
        same = jnp.where((col == row) & below, 1.0, 0.0).astype(BF16)
        return dot(same, ones_mat)

    def rank_row(at):
        col, row = owners(at)
        same = jnp.where((col == row) & above, 1.0, 0.0).astype(BF16)
        return dot(jnp.ones((8, GROUP), BF16), same)

    for update in range(2):
        row = idx_ref[16 + update : 17 + update, :]
        rank = rank_row(16 + update)[0:1]
        slot = jnp.where(owner_of(row) == p_f, rank, -1.0)
        pick = jnp.where(iota((CAP, GROUP), 0) == slot, 1.0, 0.0).astype(BF16)
        col = idxt_ref[:, 16 + update : 17 + update] - p_f * LOCAL
        hot = jnp.where(iota((GROUP, LOCAL), 1) == col, 1.0, 0.0).astype(BF16)
        place = dot(pick, hot).astype(BF16)
        g_snd[update] = dot(place, x_ref[...]).astype(BF16)

    pl.semaphore_wait(barrier, PTS + ROWS - 2)

    def to_pts(src_of, dst, sem):
        for step, hop in farthest_first:
            peer = peer_y[step] + peer_z[hop]
            pltpu.make_async_remote_copy(
                src_ref=src_of(peer), dst_ref=dst.at[me_p],
                send_sem=send_sem.at[sem], recv_sem=recv_sem.at[sem],
                device_id={"pts": peer}, device_id_type=MESH,
            ).start()
        expect(sem, dst.at[pl.ds(0, PTS - 1)])

    def to_rows(buf, sem):
        def send(hop, carry):
            peer = lax.rem(me_r + hop, ROWS)
            pltpu.make_async_remote_copy(
                src_ref=buf.at[me_r], dst_ref=buf.at[me_r],
                send_sem=send_sem.at[sem], recv_sem=recv_sem.at[sem],
                device_id={"rows": peer}, device_id_type=MESH,
            ).start()
            return carry

        lax.fori_loop(1, ROWS, send, 0)
        expect(sem, buf.at[pl.ds(0, ROWS - 1)])

    G, RS0, RS1, AX, DS, FX, FC = 0, 2, 3, 4, 6, 8, 10
    for update in range(2):
        to_pts(lambda peer: g_snd.at[update], g_rcv.at[update], G + update)
        g_rcv[update, me_p] = g_snd[update]

    loads[0].wait()
    loads[1].wait()
    w_now = w_ref[...]
    z_now = z_ref[...]
    mixed = alpha_mix * z_now + (1.0 - alpha_mix) * w_now
    base = alpha_mix * (beta_keep * z_now + (1.0 - beta_keep) * mixed) + (1.0 - alpha_mix) * mixed
    mixb_ref[...] = mixed.astype(BF16)
    baseb_ref[...] = base.astype(BF16)
    loads[2].wait()
    targets = t_ref[...].astype(F32)
    for update, value in enumerate((mixed, base)):
        wanted = ridge_term * value - targets
        high = wanted.astype(BF16)
        low = (wanted - high.astype(F32)).astype(BF16)
        col = idxt_ref[:, 16 + update : 17 + update] - p_f * LOCAL
        hot = jnp.where(iota((GROUP, LOCAL), 1) == col, 1.0, 0.0).astype(BF16)
        off_ref[update] = dot(hot, high) + dot(hot, low)

    x_sq = row_norms(x_ref[...])[0:1]

    def select_group(at, group_f, update):
        col = owner_of(idxt_ref[:, at : at + 1])
        quad = jnp.floor(col * 0.25)
        chunk = mod4(col - 4.0 * quad + group_f)
        slot = rank_col(at) + (quad * 128.0 + chunk * SLOTS)
        for block in range(ROWS):
            hit = iota((GROUP, 128), 1) + 128.0 * block == slot
            sel_ref[at, :, block * 128 : (block + 1) * 128] = jnp.where(hit, 1.0, 0.0).astype(BF16)

    for update in range(2):
        for group in range(ROWS):
            select_group(update * ROWS + group, float(group), update)

    my_quad = me_p // 4
    my_kind = p_f - 4.0 * my_quad.astype(F32)
    chunk_of = jnp.floor(iota((8, 128), 1) * (1.0 / SLOTS))
    places_ref[...] = jnp.zeros_like(places_ref)
    for update in range(2):
        for half in range(2):
            total = jnp.zeros((8, 128), F32)
            for part in range(4):
                group = half * 4 + part
                at = update * ROWS + group
                row = idx_ref[at : at + 1, :]
                inner = row - LOCAL * owner_of(row)
                upper = jnp.floor(inner * (1.0 / 32.0))
                lhs = jnp.concatenate(
                    [upper, inner - 32.0 * upper, jnp.ones_like(row), jnp.zeros((5, GROUP), F32)],
                    axis=0,
                ).astype(BF16)
                block = sel_ref[at, :, pl.ds(pl.multiple_of(my_quad * 128, 128), 128)]
                found = dot(lhs, block)
                total = jnp.where(chunk_of == mod4(my_kind + part), found, total)
            point = 32.0 * total[0:1] + total[1:2] - (1.0 - total[2:3])
            places_ref[update : update + 1, half * 128 : (half + 1) * 128] = point

    slots_iota = iota((GROUP, PTS * CAP), 1)
    for update in range(2):
        col = owner_of(idxt_ref[:, 16 + update : 17 + update])
        slot = rank_col(16 + update)[:, 0:1] + col * CAP
        own_sel_ref[update] = jnp.where(slots_iota == slot, 1.0, 0.0).astype(BF16)
        for half in range(2):
            at = 18 + update * 2 + half
            col = idxt_ref[:, at : at + 1]
            for group in range(ROWS):
                hit = iota((GROUP, GROUP), 1) + float(group * GROUP) == col
                pivot_sel_ref[update, half, :, group * GROUP : (group + 1) * GROUP] = jnp.where(
                    hit, 1.0, 0.0
                ).astype(BF16)

    def own_features(update):
        arrive(G + update)
        rows = dot(own_sel_ref[update], g_rcv[update].reshape(PTS * CAP, 128)).astype(BF16)
        feats_ref[update, core, chip] = rows
        for hop in range(1, 4):
            pltpu.make_async_remote_copy(
                src_ref=feats_ref.at[update, core, chip],
                dst_ref=feats_ref.at[update, core, chip],
                send_sem=send_sem.at[FX + update], recv_sem=recv_sem.at[FX + update],
                device_id={"rows": lax.rem(me_r + 2 * hop, ROWS)}, device_id_type=MESH,
            ).start()
        expect(FX + update, feats_ref.at[update, core, pl.ds(0, 3)])
        return rows

    def share_with_core(update):
        arrive(FX + update)
        pltpu.make_async_remote_copy(
            src_ref=feats_ref.at[update, core], dst_ref=feats_ref.at[update, core],
            send_sem=send_sem.at[FC + update], recv_sem=recv_sem.at[FC + update],
            device_id={"rows": chip * 2 + 1 - core}, device_id_type=MESH,
        ).start()
        expect(FC + update, feats_ref.at[update, core])

    def group_rows(update, group):
        return feats_ref[update, lax.rem(group, 2), group // 2]

    def partial_rows(rows, coefs, offset):
        tile = kernel_tile(rows, x_ref[...], x_sq)
        return dot(tile, coefs) + offset

    def put_pieces(dst, value):
        flipped = jnp.transpose(value)
        for piece in range(PTS):
            dst[piece] = stack(flipped[piece * 8 : piece * 8 + 8]).astype(BF16)

    rows0 = own_features(0)
    put_pieces(rs0_snd, partial_rows(rows0, mixb_ref[...], off_ref[0]))
    to_pts(lambda peer: rs0_snd.at[peer], rs0_rcv, RS0)
    rs0_rcv[me_p] = rs0_snd[me_p]

    rows1 = own_features(1)
    put_pieces(rs1_snd, partial_rows(rows1, baseb_ref[...], off_ref[1]))
    to_pts(lambda peer: rs1_snd.at[peer], rs1_rcv, RS1)
    rs1_rcv[me_p] = rs1_snd[me_p]

    def make_factor(update):
        arrive(FC + update)
        pivots = []
        for half in range(2):
            total = jnp.zeros((GROUP, 128), F32)
            for group in range(ROWS):
                hot = pivot_sel_ref[update, half, :, group * GROUP : (group + 1) * GROUP]
                total = total + dot(hot, feats_ref[update, group % 2, group // 2])
            pivots.append(total.astype(BF16))
        pivots = jnp.concatenate(pivots, axis=0)
        pivots_sq = row_norms(pivots)[0:1]

        def body(group, carry):
            at = pl.ds(pl.multiple_of(group * GROUP, GROUP), GROUP)
            factor_ref[update, at, :] = kernel_tile(group_rows(update, group), pivots, pivots_sq)
            return carry

        lax.fori_loop(0, ROWS, body, 0)

    def sum_pieces(rcv):
        total = rcv[0].astype(F32)
        for piece in range(1, PTS):
            total = total + rcv[piece].astype(F32)
        return total

    def share_rows(at, value):
        ax_ref[at, me_r] = value.astype(BF16)
        to_rows(ax_ref.at[at], AX + at)

    def whole_rows(at):
        arrive(AX + at)
        parts = []
        for group in range(ROWS):
            parts += unstack(ax_ref[at, group].astype(F32))
        return jnp.concatenate(parts, axis=1)

    rows1_sq = row_norms(rows1)[0:1]
    row1 = idx_ref[17:18, :]

    def cross_part(kind):
        for at in range(4):
            tile = kernel_tile(feats_ref[0, kind, at], rows1, rows1_sq)
            col = jnp.where(
                kind == 0, idxt_ref[:, 2 * at : 2 * at + 1], idxt_ref[:, 2 * at + 1 : 2 * at + 2]
            )
            same = jnp.where(col == row1, ridge_term, 0.0)
            rows = pl.ds(pl.multiple_of((2 * at + kind) * GROUP, GROUP), GROUP)
            cross_ref[rows, :] = (tile.astype(F32) + same).astype(BF16)

    share_with_core(0)
    cross_part(core)
    arrive(RS0)
    share_rows(0, sum_pieces(rs0_rcv))
    make_factor(0)
    share_with_core(1)
    cross_part(1 - core)
    loads[3].wait()

    def step_of(update, resid):
        proj = dot(resid.astype(BF16), factor_ref[update])
        lifted = dot(proj.astype(BF16), core_ref[update], NT).astype(BF16)
        return (resid - dot(lifted, factor_ref[update], NT)).astype(BF16)

    def send_steps(update, step):
        chunk_at = jnp.floor(iota((8, 128), 1) * (1.0 / SLOTS))
        for pair in range(4):
            cut = slice(pair * 256, pair * 256 + 256)
            found = [
                dot(
                    step[:, group * GROUP : (group + 1) * GROUP],
                    sel_ref[update * ROWS + group, :, cut],
                )
                for group in range(ROWS)
            ]
            for at in range(8):
                owner = pair * 8 + at
                halves = []
                for half in range(2):
                    total = jnp.zeros((8, 128), F32)
                    for part in range(4):
                        lanes = slice(at // 4 * 128, at // 4 * 128 + 128)
                        piece = found[half * 4 + part][:, lanes]
                        total = jnp.where(chunk_at == float((owner + part) % 4), piece, total)
                    halves.append(total)
                d_snd[update, owner] = jnp.concatenate(halves, axis=0).astype(BF16)
        to_pts(lambda peer: d_snd.at[update].at[peer], d_rcv.at[update], DS + update)
        d_rcv[update, me_p] = d_snd[update, me_p]

    def received(update):
        arrive(DS + update)
        halves = []
        for half in range(2):
            cut = slice(half * 8, half * 8 + 8)
            halves.append(
                jnp.concatenate(
                    [d_rcv[update, piece].astype(F32)[cut] for piece in range(PTS)], axis=0
                )
            )
        return jnp.concatenate(halves, axis=1).astype(BF16)

    step0 = step_of(0, whole_rows(0))
    drop = alpha_mix * step_size * momentum_gain + (1.0 - alpha_mix) * step_size
    change = dot(step0, cross_ref[...]) * drop
    arrive(RS1)
    share_rows(1, sum_pieces(rs1_rcv) - stack(change))
    send_steps(0, step0)
    make_factor(1)
    step1 = step_of(1, whole_rows(1))
    send_steps(1, step1)

    steps0 = received(0)
    for part in range(4):
        cut = slice(part * 256, part * 256 + 256)
        current, momentum_now = apply_update(
            w_ref[cut, :], z_ref[cut, :], steps0, places_ref[0:1, :], part * 256.0
        )
        w_ref[cut, :] = current
        z_ref[cut, :] = momentum_now
    stores = [
        pltpu.make_async_copy(src, dst, load_sem.at[at])
        for at, (src, dst) in enumerate([(w_ref, w_mid), (z_ref, z_mid)])
    ]
    for store in stores:
        store.start()
    steps_ref[...] = received(1)

    for store in stores:
        store.wait()
    for sem, ref in sent:
        wait_bytes(ref, send_sem.at[sem])


def apply_kernel(
    w_ref, z_ref, steps_hbm, places_hbm, w_out, z_out,
    w_now, z_now, steps_ref, places_ref, small_sem, load_sem, store_sem,
):
    tile = w_now.shape[0] // STORES
    loads = []
    stores = []
    small = [
        pltpu.make_async_copy(steps_hbm, steps_ref, small_sem.at[0]),
        pltpu.make_async_copy(places_hbm, places_ref, small_sem.at[1]),
    ]
    for load in small:
        load.start()
    for part in range(STORES):
        cut = pl.ds(part * tile, tile)
        for at, (src, dst) in enumerate([(w_ref, w_now), (z_ref, z_now)]):
            loads.append(pltpu.make_async_copy(src.at[cut], dst.at[cut], load_sem.at[at, part]))
            loads[-1].start()
    for load in small:
        load.wait()
    for part in range(STORES):
        cut = pl.ds(part * tile, tile)
        loads[2 * part].wait()
        loads[2 * part + 1].wait()
        current, momentum_now = apply_update(
            w_now[cut, :], z_now[cut, :], steps_ref[...], places_ref[1:2, :], float(part * tile)
        )
        w_now[cut, :] = current
        z_now[cut, :] = momentum_now
        for at, (src, dst) in enumerate([(w_now, w_out), (z_now, z_out)]):
            stores.append(pltpu.make_async_copy(src.at[cut], dst.at[cut], store_sem.at[at, part]))
            stores[-1].start()
    for store in stores:
        store.wait()


def shards(features, targets, coefficients, momentum, block_index, pivot_index, nystrom_core):
    vmem = pl.BlockSpec(memory_space=pltpu.VMEM)
    anywhere = pl.BlockSpec(memory_space=pl.ANY)
    hbm = pl.BlockSpec(memory_space=pltpu.HBM)
    w_mid, z_mid, steps, places = pl.pallas_call(
        block_kernel,
        out_shape=(
            jax.ShapeDtypeStruct(coefficients.shape, F32),
            jax.ShapeDtypeStruct(momentum.shape, F32),
            jax.ShapeDtypeStruct((256, GROUP), BF16),
            jax.ShapeDtypeStruct((8, GROUP), F32),
        ),
        in_specs=[hbm] * 7,
        out_specs=(anywhere, anywhere, vmem, vmem),
        scratch_shapes=[
            pltpu.VMEM(block_index.shape, jnp.int32),
            pltpu.VMEM(pivot_index.shape, jnp.int32),
            pltpu.VMEM(features.shape, BF16),
            pltpu.VMEM((128, GROUP), F32),
            pltpu.VMEM((GROUP, 128), F32),
            pltpu.VMEM((LOCAL, 256), F32),
            pltpu.VMEM((LOCAL, 256), F32),
            pltpu.VMEM((LOCAL, 256), BF16),
            pltpu.VMEM((2, 512, 512), BF16),
            pltpu.SemaphoreType.DMA((7,)),
            pltpu.VMEM((16, GROUP, PTS * SLOTS), BF16),
            pltpu.VMEM((2, GROUP, PTS * CAP), BF16),
            pltpu.VMEM((2, 2, GROUP, ROWS * GROUP), BF16),
            pltpu.VMEM((2, CAP, 128), BF16),
            pltpu.VMEM((2, PTS, CAP, 128), BF16),
            pltpu.VMEM((2, 2, 4, GROUP, 128), BF16),
            pltpu.VMEM((2, ROWS * GROUP, 512), BF16),
            pltpu.VMEM((ROWS * GROUP, GROUP), BF16),
            pltpu.VMEM((LOCAL, 256), BF16),
            pltpu.VMEM((LOCAL, 256), BF16),
            pltpu.VMEM((2, GROUP, 256), F32),
            pltpu.VMEM((PTS, 16, 128), BF16),
            pltpu.VMEM((PTS, 16, 128), BF16),
            pltpu.VMEM((PTS, 16, 128), BF16),
            pltpu.VMEM((PTS, 16, 128), BF16),
            pltpu.VMEM((2, ROWS, 16, 128), BF16),
            pltpu.VMEM((2, PTS, 16, 128), BF16),
            pltpu.VMEM((2, PTS, 16, 128), BF16),
            pltpu.SemaphoreType.DMA((12,)),
            pltpu.SemaphoreType.DMA((12,)),
        ],
        compiler_params=pltpu.CompilerParams(
            collective_id=0, has_side_effects=True, vmem_limit_bytes=VMEM_BYTES
        ),
        name="block_steps",
    )(block_index, pivot_index, features, coefficients, momentum, targets, nystrom_core)

    return pl.pallas_call(
        apply_kernel,
        out_shape=(
            jax.ShapeDtypeStruct(coefficients.shape, F32),
            jax.ShapeDtypeStruct(momentum.shape, F32),
        ),
        in_specs=[hbm, hbm, hbm, hbm],
        out_specs=(hbm, hbm),
        scratch_shapes=[
            pltpu.VMEM((LOCAL, 256), F32),
            pltpu.VMEM((LOCAL, 256), F32),
            pltpu.VMEM((256, GROUP), BF16),
            pltpu.VMEM((8, GROUP), F32),
            pltpu.SemaphoreType.DMA((2,)),
            pltpu.SemaphoreType.DMA((2, STORES)),
            pltpu.SemaphoreType.DMA((2, STORES)),
        ],
        compiler_params=pltpu.CompilerParams(vmem_limit_bytes=VMEM_BYTES),
        name="apply_steps",
    )(w_mid, z_mid, steps, places)


def solution(mesh):
    in_specs = (P("pts", None), P("pts", None), P("pts", None), P("pts", None), P(), P(), P())
    out_specs = (P("pts", None), P("pts", None))
    return jax.shard_map(shards, mesh=mesh, in_specs=in_specs, out_specs=out_specs, check_vma=False)
```
